256 devices in a mesh: seq: 128 (over x_hi, y, z, core), fsdp: 2 (over x_lo).
Axes of the slice: x: 4 (x_hi: 2, x_lo: 2; x = x_hi * 2 + x_lo), y: 4, z: 8, core: 2. Of those that a mesh axis runs over, the one named last changes fastest.
Arguments:
- dna_embed: bfloat16 [2, 32768, 1024], P('fsdp', 'seq'), may hold values from -60 to 60
- site_owner: int32 [2, 32768, 1], P('fsdp', 'seq'), may hold values from 0 to 127; in each aligned block of 256 rows (0 to 255, 256 to 511, ..., all dimensions but the last counted through in order) at most 4 rows name the same one
- site_row: int32 [2, 32768], P('fsdp', 'seq'), may hold values from 0 to 2047
- variant_table: bfloat16 [262144, 1024], P('seq'), may hold values from -6 to 6
- norm_gain: float32 [1024], replicated, may hold values from 0.1 to 1.9
- conv_weight: bfloat16 [7, 1024], replicated, may hold values from -2.390625 to 2.390625
- qkv_weight: bfloat16 [1024, 3072], P(None, 'fsdp'), may hold values from -4 to 4
- out_weight: bfloat16 [1024, 1024], P(None, 'fsdp'), may hold values from -0.1875 to 0.1875
- attn_gain: float32 [1024], replicated, may hold values from 0.1 to 1.9
Outputs:
- mixed: bfloat16 [2, 32768, 1024], P('fsdp', 'seq')
The draws below stay inside these ranges and needn't reach their ends.
Inputs may be any that keep to these rules, and one draw needn't show every extreme that they name: `site_owner`: in each haplotype the 256 positions of one device name one site range at most 4 times, and some site range exactly 4 times.
All inputs are finite; a program needn't handle non-finite values.
Results may differ from the reference program's by a relative error of at most 0.0075.
The reference program's roundings to bfloat16 on the way (of `site_embed`, `normed`, `conv_out`, `qkv`, `probs` and `attn_normed`) count: a program that leaves them out, or rounds other values in their place, can miss the bound.
Values may be sent and summed in bfloat16 or wider, within the bound.
No kernel may reach another device: no remote copies, remote signals or barrier semaphores. Data moves between devices by JAX's collectives and lax.ppermute only.
A program may use at most 128 MiB of HBM per device.

```python
import math
import jax
import jax.numpy as jnp
import numpy as np
from jax import lax

D = 1024
HEADS = 16
HEAD = 64
CONV = 7
WINDOW = 2048
L_DEV = 256
SITES_DEV = 2048
HAPS = 2
SEQ = 32768
SITES = 262144
CAP = 4
N_SEQ = 128


def draw_dna_embed(key, part):
    key_base, key_rows, key_cols = jax.random.split(key, 3)
    shape = (HAPS, SEQ, D)
    base = jnp.clip(jax.random.normal(key_base, shape, jnp.float32), -6.0, 6.0)
    row_scale = jnp.exp(jax.random.uniform(key_rows, (HAPS, SEQ, 1), jnp.float32, 0.0, math.log(10.0)))
    col_scale = jnp.exp(jax.random.uniform(key_cols, (D,), jnp.float32, 0.0, math.log(10.0)))
    return (base * row_scale * col_scale * 0.1).astype(jnp.bfloat16)


def draw_qkv_weight(key, part):
    key_base = jax.random.fold_in(key, 0)
    base = jnp.clip(jax.random.normal(key_base, (D, 3 * D), jnp.float32), -6.0, 6.0) * D ** (-0.5)
    return base.astype(jnp.bfloat16)


def with_ends(entries, rng, low, top_value):
    extent = entries.shape
    index_at = [jax.random.randint(jax.random.fold_in(rng, axis), (), 0, extent[axis]) for axis in range(len(extent))]
    entries = entries.at[tuple(index_at)].set(low)
    longest = extent.index(max(extent))
    index_at[longest] = (index_at[longest] + 1) % extent[longest]
    return entries.at[tuple(index_at)].set(top_value)


def block_levels(key, dims, pieces, low, high):
    level, own = 1.0, jax.random.fold_in(key, 6)
    for position, blocks in pieces:
        draws = jnp.exp(jax.random.uniform(jax.random.fold_in(own, position), (blocks,), jnp.float32, low / len(pieces), high / len(pieces)))
        level = level * jnp.repeat(draws, dims[position] // blocks).reshape([-1 if axis == position else 1 for axis in range(len(dims))])
    return level


def routed_block(stream_key, own, number, rows, count, top, limit, lean):
    sequence = jax.random.permutation(stream_key, count)
    crowded, common = shares(count, rows * top, limit, lean, True), shares(count, rows * top, limit, lean, False)
    places = jnp.arange(count)

    def named(lengths, rotation):
        used = int((lengths > 0).sum())
        fixed = max(1, used // 4)
        passed = fixed + (places - fixed + rotation * (used - fixed)) % max(1, count - fixed)
        return jnp.zeros((count,), jnp.int32).at[sequence[jnp.where(places < fixed, places, passed)]].set(jnp.asarray(lengths, jnp.int32))

    lengths = jnp.where(number % 4 == 0, named(crowded, number // 4), named(common, number - number // 4 - 1))
    mixed = jax.random.permutation(jax.random.fold_in(own, 3), count)
    giver, sink = mixed[0:count // 2 * 2:2], mixed[1:count // 2 * 2:2]
    room = jnp.minimum(lengths[giver] - 1, limit - lengths[sink]) // 2
    room = jnp.where((giver == sequence[0]) | (sink == sequence[0]) | (lengths[sink] == 0), 0, jnp.maximum(room, 0))
    passed = jax.random.randint(jax.random.fold_in(own, 4), (count // 2,), 0, 1 << 20) % (room + 1)
    lengths = lengths.at[giver].add(-passed).at[sink].add(passed)
    members = jnp.searchsorted(jnp.cumsum(lengths), jnp.arange(rows * top), side="right").astype(jnp.int32)
    listing = members.reshape(top, rows).T
    listing = listing[jax.random.permutation(jax.random.fold_in(own, 1), rows)]
    rotation = jax.random.randint(jax.random.fold_in(own, 2), (rows, 1), 0, top)
    return jnp.take_along_axis(listing, (jnp.arange(top)[None, :] + rotation) % top, axis=1)


def shares(amount, total, reach, skew, full):
    loads = [(1 << 20) // math.isqrt(grade ** skew) + 1 for grade in range(1, amount + 1)]
    largest = reach if full else min(reach, max(-(-total // amount), total * loads[0] // sum(loads)))
    least = 1 if total - largest >= amount - 1 else 0
    holding, surplus = [largest] + [least] * (amount - 1), total - largest - least * (amount - 1)
    while surplus > 0:
        candidates = [i for i in range(1, amount) if holding[i] < largest] or [i for i in range(1, amount) if holding[i] < reach]
        mass, budget = sum([loads[i] for i in candidates]), surplus
        for i in candidates:
            extra = min(reach - holding[i], max(1, budget * loads[i] // mass), surplus)
            holding[i] = holding[i] + extra
            surplus = surplus - extra
    return np.array(holding)


def normal_values(own_key, extent, deviation, bound, cuts=(), kind=jnp.bfloat16):
    entries = jax.random.normal(own_key, extent, jnp.float32) * deviation
    if len(cuts) > 0:
        entries = block_levels(own_key, extent, cuts, -0.22, 0.18) * entries
    return jnp.clip(entries, min=-bound, max=bound).astype(kind)


def setup_inputs(seed: int = 0) -> dict:
    arg_keys = jax.random.split(jax.random.key(seed), 10)
    dna_embed = draw_dna_embed(jax.random.fold_in(arg_keys[9], 71), 0)
    site_owner_keys = jax.random.split(jax.random.fold_in(arg_keys[1], 1), HAPS * SEQ // L_DEV)
    site_owner_turns = jax.random.permutation(jax.random.fold_in(arg_keys[1], 3), HAPS * SEQ // L_DEV)
    site_owner = jax.vmap(lambda own, number: routed_block(jax.random.fold_in(arg_keys[1], 2), own, number, L_DEV, N_SEQ, 1, CAP, 2))(site_owner_keys, site_owner_turns).reshape((HAPS, SEQ, 1))
    site_row = with_ends(jax.random.randint(arg_keys[2], (HAPS, SEQ), 0, SITES_DEV), jax.random.fold_in(arg_keys[2], 1), 0, SITES_DEV - 1).astype(jnp.int32)
    variant_table = normal_values(arg_keys[3], (SITES, D), 1.0, 6.0, ((0, 128),))
    norm_gain = jnp.clip(1.0 + 0.18 * jax.random.normal(arg_keys[4], (D,), jnp.float32), 0.1, 1.9)
    conv_weight = normal_values(arg_keys[5], (CONV, D), 0.4, 2.390625)
    qkv_weight = draw_qkv_weight(jax.random.fold_in(arg_keys[9], 71), 0)
    out_weight = normal_values(arg_keys[7], (D, D), D ** -0.5, 0.1875, ((1, 2),))
    attn_gain = jnp.clip(1.0 + 0.18 * jax.random.normal(arg_keys[8], (D,), jnp.float32), 0.1, 1.9)
    return dict(dna_embed=dna_embed, site_owner=site_owner, site_row=site_row, variant_table=variant_table, norm_gain=norm_gain, conv_weight=conv_weight, qkv_weight=qkv_weight, out_weight=out_weight, attn_gain=attn_gain)


EPSILON = 1e-05

def rms_scale(values, gain):
    return values * lax.rsqrt(lax.optimization_barrier(jnp.mean(values * values, axis=-1, keepdims=True)) + EPSILON) * gain

def window_block(query, key_value, block_index):
    start = (block_index * L_DEV).astype(jnp.int32)
    q_block = lax.dynamic_slice_in_dim(query, start, L_DEV, 0)
    k_block = lax.dynamic_slice_in_dim(key_value, start, WINDOW + L_DEV, 0)
    q_where = start + jnp.arange(L_DEV, dtype=jnp.int32)
    k_where = start - WINDOW + jnp.arange(WINDOW + L_DEV, dtype=jnp.int32)
    allowed = (k_where[None, :] <= q_where[:, None]) & (k_where[None, :] > q_where[:, None] - WINDOW) & (k_where[None, :] >= 0)
    q_heads = q_block.reshape(L_DEV, HEADS, HEAD).astype(jnp.float32)
    k_heads = k_block[:, :D].reshape(WINDOW + L_DEV, HEADS, HEAD).astype(jnp.float32)
    v_heads = k_block[:, D:].reshape(WINDOW + L_DEV, HEADS, HEAD).astype(jnp.float32)
    scores = jnp.einsum('qhd,khd->hqk', q_heads, k_heads) * HEAD ** (-0.5)
    scores = jnp.where(allowed[None, :, :], scores, -jnp.inf)
    highest = lax.optimization_barrier(jnp.max(scores, axis=-1, keepdims=True))
    expo = jnp.exp(scores - highest)
    probs = (expo / lax.optimization_barrier(jnp.sum(expo, axis=-1, keepdims=True))).astype(jnp.bfloat16)
    attended = jnp.einsum('hqk,khd->qhd', probs.astype(jnp.float32), v_heads)
    return attended.reshape(L_DEV, D)

def one_haplotype(tokens_in, owner_ids, row_ids, variant_table, norm_gain, conv_weight, qkv_weight, out_weight, attn_gain):
    site_embed = variant_table[owner_ids * SITES_DEV + row_ids]
    resid = tokens_in.astype(jnp.float32) + site_embed.astype(jnp.float32)
    normed = rms_scale(resid, norm_gain).astype(jnp.bfloat16)
    padded = jnp.pad(normed, ((CONV - 1, 0), (0, 0)))
    conv_sum = jnp.zeros((SEQ, D), jnp.float32)
    for tap in range(CONV):
        conv_sum = conv_sum + conv_weight[tap].astype(jnp.float32) * padded[CONV - 1 - tap:CONV - 1 - tap + SEQ].astype(jnp.float32)
    conv_out = conv_sum.astype(jnp.bfloat16)
    qkv = jnp.dot(conv_out, qkv_weight, preferred_element_type=jnp.float32).astype(jnp.bfloat16)
    query = qkv[:, :D]
    key_value = jnp.pad(qkv[:, D:], ((WINDOW, 0), (0, 0)))
    blocks = lax.map(lambda index: window_block(query, key_value, index), jnp.arange(SEQ // L_DEV, dtype=jnp.int32))
    attended = blocks.reshape(SEQ, D)
    attn_normed = rms_scale(attended, attn_gain).astype(jnp.bfloat16)
    return jnp.dot(attn_normed, out_weight, preferred_element_type=jnp.float32).astype(jnp.bfloat16)

def reference(dna_embed, site_owner, site_row, variant_table, norm_gain, conv_weight, qkv_weight, out_weight, attn_gain):
    results = []
    for haplotype in range(HAPS):
        results.append(one_haplotype(dna_embed[haplotype], site_owner[haplotype, :, 0], site_row[haplotype], variant_table, norm_gain, conv_weight, qkv_weight, out_weight, attn_gain))
    return jnp.stack(results, axis=0)
```

```python
import jax
import jax.numpy as jnp
from jax import lax
from jax.experimental import pallas as pl
from jax.experimental.pallas import tpu as pltpu
from jax.sharding import PartitionSpec as P

HEAD = 64
WINDOW = 2048
EPSILON = 1e-05
ROWS = 256
D = 1024
HALF = 512
OWNERS = 128
SLOTS = 4
HOPS = 4
BLOCKS = 2 * (HOPS + 1)
SPAN = WINDOW // ROWS + 1
LOG2E = 1.4426950408889634

bf16 = jnp.bfloat16
f32 = jnp.float32


def vmem():
    return pl.BlockSpec(memory_space=pltpu.VMEM)


def anywhere():
    return pl.BlockSpec(memory_space=pl.ANY)


def cost(flops, moved):
    return pl.CostEstimate(flops=flops, bytes_accessed=moved, transcendentals=0)


def request_kernel(owner_col, owner_row, row_row, table, slot):
    oc, orow = owner_col[...], owner_row[...]
    later = lax.broadcasted_iota(jnp.int32, (ROWS, ROWS), 0) < lax.broadcasted_iota(jnp.int32, (ROWS, ROWS), 1)
    rank = jnp.sum(jnp.where((oc == orow) & later, 1, 0), axis=0, keepdims=True)
    mine = lax.broadcasted_iota(jnp.int32, (OWNERS, ROWS), 0) == orow
    lane = lax.broadcasted_iota(jnp.int32, (OWNERS, 128), 1)
    out = jnp.zeros((OWNERS, 128), jnp.int32)
    for k in range(SLOTS):
        column = jnp.sum(jnp.where(mine & (rank == k), row_row[...], 0), axis=1, keepdims=True)
        out = jnp.where(lane == k, column, out)
    table[...] = out
    slot[...] = orow * SLOTS + rank


def norm_kernel(fetched, slot, dna, gain, normed):
    index = slot[...]
    pick = (lax.broadcasted_iota(jnp.int32, (OWNERS * SLOTS, ROWS), 0) == index).astype(f32).astype(bf16)
    site = lax.dot_general(pick, fetched[...], (((0,), (0,)), ((), ())), preferred_element_type=f32)
    resid = dna[...].astype(f32) + site
    mean = jnp.mean(resid * resid, axis=1, keepdims=True)
    normed[...] = (resid * lax.rsqrt(mean + EPSILON) * gain[...]).astype(bf16)


def conv_kernel(normed, rim, taps, out, padded):
    padded[pl.ds(2, 6), :] = rim[...].astype(f32)
    padded[pl.ds(8, ROWS), :] = normed[...].astype(f32)
    total = jnp.zeros((ROWS, D), f32)
    for tap in range(7):
        total = total + taps[pl.ds(tap, 1), :].astype(f32) * padded[pl.ds(8 - tap, ROWS), :]
    out[...] = total.astype(bf16)


def attend_kernel(*refs):
    own, other = refs[0 : HOPS + 1], refs[HOPS + 1 : 2 * HOPS + 2]
    wq, wk, wv, mine, theirs, xs, qs, ks, vs, mask, sc0, sc1, sems = refs[2 * HOPS + 2 :]
    seq = lax.axis_index("seq")
    par = lax.rem(seq, 2)
    chip = seq // 2
    copies = []
    for k in range(HOPS + 1):
        base = 2 * (HOPS - k) * ROWS
        here = pl.multiple_of(base + par * ROWS, ROWS)
        there = pl.multiple_of(base + (1 - par) * ROWS, ROWS)
        copies.append(pltpu.make_async_copy(own[k], xs.at[pl.ds(here, ROWS), :], sems.at[2 * k]))
        copies.append(pltpu.make_async_copy(other[k], xs.at[pl.ds(there, ROWS), :], sems.at[2 * k + 1]))
    for copy in copies:
        copy.start()
    row = lax.broadcasted_iota(jnp.int32, (ROWS, ROWS), 0)
    col = lax.broadcasted_iota(jnp.int32, (ROWS, ROWS), 1)
    for qb in range(2):
        for kb in range(SPAN):
            live = chip * 2 - 2 * HOPS + qb + kb >= 0
            ok = jnp.broadcast_to(live, (ROWS, ROWS))
            if kb == 0:
                ok = ok & (col > row)
            if kb == SPAN - 1:
                ok = col <= row
            mask[qb, :, pl.ds(kb * ROWS, ROWS)] = jnp.where(ok, 0.0, -jnp.inf).astype(f32)
    for copy in copies:
        copy.wait()

    def project(b, carry):
        at = pl.ds(pl.multiple_of(b * ROWS, ROWS), ROWS)
        x = xs[at, :]
        ks[at, :] = jnp.dot(x, wk[...], preferred_element_type=f32).astype(bf16)
        vs[at, :] = jnp.dot(x, wv[...], preferred_element_type=f32).astype(bf16)
        return carry

    lax.fori_loop(0, BLOCKS, project, 0)

    def project_q(b, carry):
        at = pl.ds(pl.multiple_of(b * ROWS, ROWS), ROWS)
        x = xs[pl.ds(pl.multiple_of((b + 2 * HOPS) * ROWS, ROWS), ROWS), :]
        qs[at, :] = jnp.dot(x, wq[...], preferred_element_type=f32).astype(bf16)
        return carry

    lax.fori_loop(0, 2, project_q, 0)

    lane = lax.broadcasted_iota(jnp.int32, (ROWS, 128), 1)

    def pair(step, carry):
        qb, hp = step // 4, lax.rem(step, 4)
        lanes = pl.ds(pl.multiple_of(hp * 128, 128), 128)
        q = qs[pl.ds(pl.multiple_of(qb * ROWS, ROWS), ROWS), lanes]
        outs = []
        for h, sc in ((0, sc0), (1, sc1)):
            qh = jnp.where((lane < HEAD) == (h == 0), q, jnp.zeros_like(q))
            top = None
            for kb in range(SPAN):
                at = pl.ds(pl.multiple_of((qb + kb) * ROWS, ROWS), ROWS)
                s = lax.dot_general(qh, ks[at, lanes], (((1,), (1,)), ((), ())), preferred_element_type=f32)
                s = s + mask[qb, :, pl.ds(kb * ROWS, ROWS)]
                sc[:, pl.ds(kb * ROWS, ROWS)] = s
                part = jnp.maximum(s[:, :128], s[:, 128:])
                top = part if top is None else jnp.maximum(top, part)
            top = jnp.max(top, axis=1, keepdims=True)
            total = None
            for kb in range(SPAN):
                e = jnp.exp2((sc[:, pl.ds(kb * ROWS, ROWS)] - top) * (LOG2E * HEAD ** (-0.5)))
                sc[:, pl.ds(kb * ROWS, ROWS)] = e
                part = e[:, :128] + e[:, 128:]
                total = part if total is None else total + part
            inverse = 1.0 / jnp.sum(total, axis=1, keepdims=True)
            acc = None
            for kb in range(SPAN):
                at = pl.ds(pl.multiple_of((qb + kb) * ROWS, ROWS), ROWS)
                p = (sc[:, pl.ds(kb * ROWS, ROWS)] * inverse).astype(bf16)
                part = jnp.dot(p, vs[at, lanes], preferred_element_type=f32)
                acc = part if acc is None else acc + part
            outs.append(acc)
        both = jnp.where(lane < HEAD, outs[0], outs[1])

        @pl.when(qb == par)
        def _():
            mine[:, lanes] = both

        @pl.when(qb != par)
        def _():
            theirs[:, lanes] = both

        return carry

    lax.fori_loop(0, 8, pair, 0)


def out_kernel(mine, received, gain, w_here, w_there, out):
    par = lax.rem(lax.axis_index("seq"), 2)
    f = lax.axis_index("fsdp")
    a, b = mine[...], received[...]
    mean = (jnp.sum(a * a, axis=1, keepdims=True) + jnp.sum(b * b, axis=1, keepdims=True)) / D
    scale = lax.rsqrt(mean + EPSILON)
    at_a = pl.ds(pl.multiple_of(par * HALF, HALF), HALF)
    at_b = pl.ds(pl.multiple_of((1 - par) * HALF, HALF), HALF)
    na = (a * scale * gain[:, at_a]).astype(bf16)
    nb = (b * scale * gain[:, at_b]).astype(bf16)
    for w, side in ((w_here, f), (w_there, 1 - f)):
        y = jnp.dot(na, w[at_a, :], preferred_element_type=f32) + jnp.dot(nb, w[at_b, :], preferred_element_type=f32)
        out[:, pl.ds(pl.multiple_of(side * HALF, HALF), HALF)] = y.astype(bf16)


def local(dna_embed, site_owner, site_row, variant_table, norm_gain, conv_weight, qkv_weight, out_weight, attn_gain):
    count = lax.axis_size("seq")
    par = lax.rem(lax.axis_index("seq"), 2)
    f = lax.axis_index("fsdp")
    across = [(0, 1), (1, 0)]
    swap = [(i, i ^ 1) for i in range(count)]
    ahead = [(i, i + 2) for i in range(count - 2)]

    main = lax.dynamic_slice_in_dim(qkv_weight, HALF * (par + f), HALF, 1)
    aux = lax.dynamic_slice_in_dim(qkv_weight, D * (1 - f) + 256 * par, 256, 1)
    main_in = lax.ppermute(main, "fsdp", across)
    aux_in = lax.ppermute(aux, "fsdp", across)
    aux_pair = lax.ppermute(aux_in, "seq", swap)
    out_half = lax.dynamic_slice_in_dim(out_weight, HALF * par, HALF, 0)
    out_in = lax.ppermute(out_half, "fsdp", across)
    out_pair = lax.ppermute(out_in, "seq", swap)

    table, slot = pl.pallas_call(
        request_kernel,
        out_shape=(jax.ShapeDtypeStruct((OWNERS, 128), jnp.int32), jax.ShapeDtypeStruct((1, ROWS), jnp.int32)),
        in_specs=[vmem()] * 3,
        out_specs=(vmem(), vmem()),
        name="requests",
    )(site_owner[0], site_owner.reshape(1, ROWS), site_row)
    wanted = lax.all_to_all(table, "seq", split_axis=0, concat_axis=0, tiled=True)
    found = variant_table[wanted[:, :SLOTS].reshape(OWNERS * SLOTS)]
    fetched = lax.all_to_all(found, "seq", split_axis=0, concat_axis=0, tiled=True)
    normed = pl.pallas_call(
        norm_kernel,
        out_shape=jax.ShapeDtypeStruct((ROWS, D), bf16),
        in_specs=[vmem()] * 4,
        out_specs=vmem(),
        name="norm",
    )(fetched, slot, dna_embed[0], norm_gain.reshape(1, D))
    rim = lax.ppermute(normed[ROWS - 6 :], "seq", [(i, i + 1) for i in range(count - 1)])
    x = pl.pallas_call(
        conv_kernel,
        out_shape=jax.ShapeDtypeStruct((ROWS, D), bf16),
        in_specs=[vmem()] * 3,
        out_specs=vmem(),
        scratch_shapes=[pltpu.VMEM((ROWS + 8, D), f32)],
        name="conv",
    )(normed, rim, conv_weight)
    own = [x]
    for _ in range(HOPS):
        own.append(lax.ppermute(own[-1], "seq", ahead))
    other = [lax.ppermute(value, "seq", swap) for value in own]

    first = f == 0
    wq = jnp.where(first, main, main_in)
    wv = jnp.where(first, main_in, main)
    k_here = lax.dynamic_slice_in_dim(qkv_weight, D * (1 - f), HALF, 1)
    lower = jnp.where(par == 0, aux_in, aux_pair)
    upper = jnp.where(par == 0, aux_pair, aux_in)
    wk = jnp.where(par == f, k_here, jnp.concatenate([lower, upper], axis=1))
    mine, theirs = pl.pallas_call(
        attend_kernel,
        out_shape=(jax.ShapeDtypeStruct((ROWS, HALF), f32), jax.ShapeDtypeStruct((ROWS, HALF), f32)),
        in_specs=[anywhere()] * BLOCKS + [vmem()] * 3,
        out_specs=(vmem(), vmem()),
        scratch_shapes=[
            pltpu.VMEM((BLOCKS * ROWS, D), bf16),
            pltpu.VMEM((2 * ROWS, HALF), bf16),
            pltpu.VMEM((BLOCKS * ROWS, HALF), bf16),
            pltpu.VMEM((BLOCKS * ROWS, HALF), bf16),
            pltpu.VMEM((2, ROWS, SPAN * ROWS), f32),
            pltpu.VMEM((ROWS, SPAN * ROWS), f32),
            pltpu.VMEM((ROWS, SPAN * ROWS), f32),
            pltpu.SemaphoreType.DMA((BLOCKS,)),
        ],
        compiler_params=pltpu.CompilerParams(vmem_limit_bytes=48 * 2**20),
        cost_estimate=cost(12 * 10**9, 10 * 2**20),
        name="attend",
    )(*own, *other, wq, wk, wv)
    received = lax.ppermute(theirs, "seq", swap)
    w_there = jnp.concatenate(
        [jnp.where(par == 0, out_in, out_pair), jnp.where(par == 0, out_pair, out_in)], axis=0
    )
    mixed = pl.pallas_call(
        out_kernel,
        out_shape=jax.ShapeDtypeStruct((ROWS, D), bf16),
        in_specs=[vmem()] * 5,
        out_specs=vmem(),
        name="project",
    )(mine, received, attn_gain.reshape(1, D), out_weight, w_there)
    return mixed[None]


def solution(mesh):
    in_specs = (
        P("fsdp", "seq", None),
        P("fsdp", "seq", None),
        P("fsdp", "seq"),
        P("seq", None),
        P(),
        P(),
        P(None, "fsdp"),
        P(None, "fsdp"),
        P(),
    )
    return jax.shard_map(local, mesh=mesh, in_specs=in_specs, out_specs=P("fsdp", "seq", None), check_vma=False)
```

```python
import jax
import jax.numpy as jnp
from jax import lax
from jax.experimental import pallas as pl
from jax.experimental.pallas import tpu as pltpu
from jax.sharding import PartitionSpec as P

HEAD = 64
WINDOW = 2048
EPSILON = 1e-05
ROWS = 256
D = 1024
HALF = 512
OWNERS = 128
SLOTS = 4
HOPS = 4
SPAN = WINDOW // ROWS + 1
LOG2E = 1.4426950408889634

bf16 = jnp.bfloat16
f32 = jnp.float32


def vmem():
    return pl.BlockSpec(memory_space=pltpu.VMEM)


def anywhere():
    return pl.BlockSpec(memory_space=pltpu.HBM)


def limit(mib):
    return pltpu.CompilerParams(vmem_limit_bytes=mib * 2**20)


def cost(flops, moved):
    return pl.CostEstimate(flops=flops, bytes_accessed=moved, transcendentals=0)


def slab_kernel(qkv, out, main, aux, half, sems):
    par = lax.rem(lax.axis_index("seq"), 2)
    f = lax.axis_index("fsdp")
    copies = (
        pltpu.make_async_copy(qkv.at[:, pl.ds(pl.multiple_of(HALF * (par + f), HALF), HALF)], main, sems.at[0]),
        pltpu.make_async_copy(qkv.at[:, pl.ds(pl.multiple_of(D * (1 - f) + 256 * par, 256), 256)], aux, sems.at[1]),
        pltpu.make_async_copy(out.at[pl.ds(pl.multiple_of(HALF * par, HALF), HALF), :], half, sems.at[2]),
    )
    for copy in copies:
        copy.start()
    for copy in copies:
        copy.wait()


def weight_kernel(qkv, main, main_in, aux_in, aux_pair, wq, wk, wv, sem):
    par = lax.rem(lax.axis_index("seq"), 2)
    f = lax.axis_index("fsdp")

    @pl.when(par == f)
    def _():
        copy = pltpu.make_async_copy(qkv.at[:, pl.ds(pl.multiple_of(D * (1 - f), D), HALF)], wk, sem)
        copy.start()
        copy.wait()

    @pl.when(par != f)
    def _():
        wk[:, pl.ds(pl.multiple_of(par * 256, 256), 256)] = aux_in[...]
        wk[:, pl.ds(pl.multiple_of((1 - par) * 256, 256), 256)] = aux_pair[...]

    @pl.when(f == 0)
    def _():
        wq[...] = main[...]
        wv[...] = main_in[...]

    @pl.when(f == 1)
    def _():
        wq[...] = main_in[...]
        wv[...] = main[...]


def request_kernel(owner, rows, table, slot):
    orow = owner[...]
    above = lax.broadcasted_iota(jnp.int32, (ROWS, ROWS), 0)
    along = lax.broadcasted_iota(jnp.int32, (ROWS, ROWS), 1)
    ocol = jnp.sum(jnp.where(above == along, orow, 0), axis=1, keepdims=True)
    same = ocol == orow
    rank = jnp.sum(jnp.where(same & (above < along), 1, 0), axis=0, keepdims=True)
    rank_col = jnp.sum(jnp.where(same & (along < above), 1, 0), axis=1, keepdims=True)
    mine = lax.broadcasted_iota(jnp.int32, (OWNERS, ROWS), 0) == orow
    lane = lax.broadcasted_iota(jnp.int32, (OWNERS, 128), 1)
    out = jnp.zeros((OWNERS, 128), jnp.int32)
    for k in range(SLOTS):
        column = jnp.sum(jnp.where(mine & (rank == k), rows[...], 0), axis=1, keepdims=True)
        out = jnp.where(lane == k, column, out)
    table[...] = out
    slot[...] = ocol * SLOTS + rank_col


def norm_kernel(fetched, slot, dna, gain, normed, rim):
    pick = (lax.broadcasted_iota(jnp.int32, (ROWS, OWNERS * SLOTS), 1) == slot[...]).astype(f32).astype(bf16)
    site = jnp.dot(pick, fetched[...], preferred_element_type=f32)
    resid = dna[...].astype(f32) + site
    mean = jnp.mean(resid * resid, axis=1, keepdims=True)
    out = (resid * lax.rsqrt(mean + EPSILON) * gain[...]).astype(bf16)
    normed[...] = out
    rim[...] = out[ROWS - 8 :]


def conv_kernel(normed, rim, taps, out, padded):
    padded[pl.ds(0, 8), :] = rim[...].astype(f32)
    padded[pl.ds(8, ROWS), :] = normed[...].astype(f32)

    def column(c, carry):
        lanes = pl.ds(pl.multiple_of(c * 128, 128), 128)
        weight = taps[:, lanes].astype(f32)
        for part in range(2):
            total = jnp.zeros((128, 128), f32)
            for tap in range(7):
                total = total + weight[tap : tap + 1] * padded[pl.ds(part * 128 + 8 - tap, 128), lanes]
            out[pl.ds(part * 128, 128), lanes] = total.astype(bf16)
        return carry

    lax.fori_loop(0, D // 128, column, 0)


def kv_kernel(own, other, wk, wv, kv):
    par = lax.rem(lax.axis_index("seq"), 2)
    for x, side in ((own, par), (other, 1 - par)):
        at = pl.ds(pl.multiple_of(side * ROWS, ROWS), ROWS)
        kv[at, :HALF] = jnp.dot(x[...], wk[...], preferred_element_type=f32).astype(bf16)
        kv[at, HALF:] = jnp.dot(x[...], wv[...], preferred_element_type=f32).astype(bf16)


def q_kernel(own, other, wq, q):
    par = lax.rem(lax.axis_index("seq"), 2)
    for x, side in ((own, par), (other, 1 - par)):
        at = pl.ds(pl.multiple_of(side * ROWS, ROWS), ROWS)
        q[at, :] = jnp.dot(x[...], wq[...], preferred_element_type=f32).astype(bf16)


def attend_kernel(q_ref, kv0, kv1, kv2, kv3, kv4, mine, theirs, edge, bias, sc0, sc1, done):
    kv = (kv0, kv1, kv2, kv3, kv4)
    seq = lax.axis_index("seq")
    par = lax.rem(seq, 2)
    chip = seq // 2
    row = lax.broadcasted_iota(jnp.int32, (ROWS, ROWS), 0)
    col = lax.broadcasted_iota(jnp.int32, (ROWS, ROWS), 1)
    edge[0] = jnp.where(col > row, 0.0, -jnp.inf).astype(f32)
    edge[1] = jnp.where(col <= row, 0.0, -jnp.inf).astype(f32)
    block = lax.broadcasted_iota(jnp.int32, (16, ROWS), 0)
    bias[...] = jnp.where(block + 2 * (chip - HOPS) >= 0, 0.0, -jnp.inf).astype(f32)
    lane = lax.broadcasted_iota(jnp.int32, (ROWS, 128), 1)

    def place(h, b, value):
        lanes = pl.ds(pl.multiple_of(value * HALF + (h // 2) * 128, 128), 128)
        return kv[HOPS - b // 2][(b % 2) * ROWS : (b % 2 + 1) * ROWS, lanes]

    def scores(qb, h, sc):
        lanes = pl.ds(pl.multiple_of((h // 2) * 128, 128), 128)
        q = q_ref[qb * ROWS : (qb + 1) * ROWS, lanes]
        q = jnp.where((lane // HEAD) == lax.rem(h, 2), q, jnp.zeros_like(q))
        top = None
        for kb in range(SPAN):
            s = lax.dot_general(q, place(h, qb + kb, 0), (((1,), (1,)), ((), ())), preferred_element_type=f32)
            if kb < SPAN - 1:
                s = s + bias[qb + kb : qb + kb + 1, :]
            if kb == 0:
                s = s + edge[0]
            if kb == SPAN - 1:
                s = s + edge[1]
            sc[:, kb * ROWS : (kb + 1) * ROWS] = s
            part = jnp.maximum(s[:, :128], s[:, 128:])
            top = part if top is None else jnp.maximum(top, part)
        return jnp.max(top, axis=1, keepdims=True)

    def weigh(qb, h, sc, top):
        total = None
        for kb in range(SPAN):
            e = jnp.exp2((sc[:, kb * ROWS : (kb + 1) * ROWS] - top) * (LOG2E * HEAD ** (-0.5)))
            sc[:, kb * ROWS : (kb + 1) * ROWS] = e
            part = e[:, :128] + e[:, 128:]
            total = part if total is None else total + part
        inverse = 1.0 / jnp.sum(total, axis=1, keepdims=True)
        acc = None
        for kb in range(SPAN):
            p = (sc[:, kb * ROWS : (kb + 1) * ROWS] * inverse).astype(bf16)
            part = jnp.dot(p, place(h, qb + kb, 1), preferred_element_type=f32)
            acc = part if acc is None else acc + part
        lanes = pl.ds(pl.multiple_of((h // 2) * 128, 128), 128)
        old = done[qb, :, lanes]
        done[qb, :, lanes] = jnp.where((lane // HEAD) == lax.rem(h, 2), acc, old)

    def head(h, top0):
        top1 = scores(1, h, sc1)
        weigh(0, h, sc0, top0)
        after = scores(0, jnp.minimum(h + 1, 7), sc0)
        weigh(1, h, sc1, top1)
        return after

    lax.fori_loop(0, 8, head, scores(0, 0, sc0))
    mine[...] = done[par]
    theirs[...] = done[1 - par]


def out_kernel(mine, received, gain, w_here, w_mine, w_other, out):
    par = lax.rem(lax.axis_index("seq"), 2)
    f = lax.axis_index("fsdp")
    a, b = mine[...], received[...]
    mean = (jnp.sum(a * a, axis=1, keepdims=True) + jnp.sum(b * b, axis=1, keepdims=True)) / D
    scale = lax.rsqrt(mean + EPSILON)
    at_a = pl.ds(pl.multiple_of(par * HALF, HALF), HALF)
    at_b = pl.ds(pl.multiple_of((1 - par) * HALF, HALF), HALF)
    na = (a * scale * gain[:, at_a]).astype(bf16)
    nb = (b * scale * gain[:, at_b]).astype(bf16)
    here = jnp.dot(na, w_here[at_a, :], preferred_element_type=f32)
    here = here + jnp.dot(nb, w_here[at_b, :], preferred_element_type=f32)
    there = jnp.dot(na, w_mine[...], preferred_element_type=f32)
    there = there + jnp.dot(nb, w_other[...], preferred_element_type=f32)
    out[:, pl.ds(pl.multiple_of(f * HALF, HALF), HALF)] = here.astype(bf16)
    out[:, pl.ds(pl.multiple_of((1 - f) * HALF, HALF), HALF)] = there.astype(bf16)


def local(dna_embed, site_owner, site_row, variant_table, norm_gain, conv_weight, qkv_weight, out_weight, attn_gain):
    count = lax.axis_size("seq")
    across = [(0, 1), (1, 0)]
    swap = [(i, i ^ 1) for i in range(count)]
    ahead = [(i, i + 2) for i in range(count - 2)]

    main, aux, half = pl.pallas_call(
        slab_kernel,
        out_shape=(
            jax.ShapeDtypeStruct((D, HALF), bf16),
            jax.ShapeDtypeStruct((D, 256), bf16),
            jax.ShapeDtypeStruct((HALF, HALF), bf16),
        ),
        in_specs=[anywhere()] * 2,
        out_specs=(vmem(), vmem(), vmem()),
        scratch_shapes=[pltpu.SemaphoreType.DMA((3,))],
        compiler_params=limit(4),
        name="slabs",
    )(qkv_weight, out_weight)
    main_in = lax.ppermute(main, "fsdp", across)
    aux_in = lax.ppermute(aux, "fsdp", across)
    out_in = lax.ppermute(half, "fsdp", across)
    aux_pair = lax.ppermute(aux_in, "seq", swap)
    out_pair = lax.ppermute(out_in, "seq", swap)

    table, slot = pl.pallas_call(
        request_kernel,
        out_shape=(jax.ShapeDtypeStruct((OWNERS, 128), jnp.int32), jax.ShapeDtypeStruct((ROWS, 1), jnp.int32)),
        in_specs=[vmem()] * 2,
        out_specs=(vmem(), vmem()),
        compiler_params=limit(4),
        name="requests",
    )(site_owner.reshape(1, ROWS), site_row)
    wanted = lax.all_to_all(table, "seq", split_axis=0, concat_axis=0, tiled=True)
    found = variant_table[wanted[:, :SLOTS].reshape(OWNERS * SLOTS)]
    fetched = lax.all_to_all(found, "seq", split_axis=0, concat_axis=0, tiled=True)
    normed, edge = pl.pallas_call(
        norm_kernel,
        out_shape=(jax.ShapeDtypeStruct((ROWS, D), bf16), jax.ShapeDtypeStruct((8, D), bf16)),
        in_specs=[vmem()] * 4,
        out_specs=(vmem(), vmem()),
        compiler_params=limit(10),
    name="norm",
    )(fetched, slot, dna_embed[0], norm_gain.reshape(1, D))
    rim = lax.ppermute(edge, "seq", [(i, i + 1) for i in range(count - 1)])
    x = pl.pallas_call(
        conv_kernel,
        out_shape=jax.ShapeDtypeStruct((ROWS, D), bf16),
        in_specs=[vmem()] * 3,
        out_specs=vmem(),
        scratch_shapes=[pltpu.VMEM((ROWS + 8, D), f32)],
        compiler_params=limit(6),
        name="conv",
    )(normed, rim, conv_weight)
    own = [x]
    for _ in range(HOPS):
        own.append(lax.ppermute(own[-1], "seq", ahead))
    other = []
    for hop in range(HOPS + 1):
        other.append(lax.ppermute(own[hop], "seq", swap))

    wq, wk, wv = pl.pallas_call(
        weight_kernel,
        out_shape=(jax.ShapeDtypeStruct((D, HALF), bf16),) * 3,
        in_specs=[anywhere()] + [vmem()] * 4,
        out_specs=(vmem(), vmem(), vmem()),
        scratch_shapes=[pltpu.SemaphoreType.DMA],
        compiler_params=limit(8),
        cost_estimate=cost(10**6, 6 * 2**20),
        name="weights",
    )(qkv_weight, main, main_in, aux_in, aux_pair)
    q = pl.pallas_call(
        q_kernel,
        out_shape=jax.ShapeDtypeStruct((2 * ROWS, HALF), bf16),
        in_specs=[vmem()] * 3,
        out_specs=vmem(),
        cost_estimate=cost(2 * 512 * D * HALF, 3 * 2**20),
        compiler_params=limit(6),
    name="queries",
    )(own[0], other[0], wq)
    kv = []
    for hop in range(HOPS + 1):
        kv.append(
            pl.pallas_call(
                kv_kernel,
                out_shape=jax.ShapeDtypeStruct((2 * ROWS, D), bf16),
                in_specs=[vmem()] * 4,
                out_specs=vmem(),
                cost_estimate=cost(2 * 512 * D * D, 4 * 2**20),
                compiler_params=limit(8),
    name="keys",
            )(own[hop], other[hop], wk, wv)
        )
    mine, theirs = pl.pallas_call(
        attend_kernel,
        out_shape=(jax.ShapeDtypeStruct((ROWS, HALF), f32), jax.ShapeDtypeStruct((ROWS, HALF), f32)),
        in_specs=[vmem()] * 6,
        out_specs=(vmem(), vmem()),
        scratch_shapes=[
            pltpu.VMEM((2, ROWS, ROWS), f32),
            pltpu.VMEM((16, ROWS), f32),
            pltpu.VMEM((ROWS, SPAN * ROWS), f32),
            pltpu.VMEM((ROWS, SPAN * ROWS), f32),
            pltpu.VMEM((2, ROWS, HALF), f32),
        ],
        cost_estimate=cost(5 * 10**9, 6 * 2**20),
        compiler_params=limit(16),
    name="attend",
    )(q, *kv)
    received = lax.ppermute(theirs, "seq", swap)
    mixed = pl.pallas_call(
        out_kernel,
        out_shape=jax.ShapeDtypeStruct((ROWS, D), bf16),
        in_specs=[vmem()] * 6,
        out_specs=vmem(),
        compiler_params=limit(10),
        name="project",
    )(mine, received, attn_gain.reshape(1, D), out_weight, out_in, out_pair)
    return mixed[None]


def solution(mesh):
    in_specs = (
        P("fsdp", "seq", None),
        P("fsdp", "seq", None),
        P("fsdp", "seq"),
        P("seq", None),
        P(),
        P(),
        P(None, "fsdp"),
        P(None, "fsdp"),
        P(),
    )

    return jax.shard_map(local, mesh=mesh, in_specs=in_specs, out_specs=P("fsdp", "seq", None), check_vma=False)
```

```python
import functools

import jax
import jax.numpy as jnp
from jax import lax
from jax.experimental import pallas as pl
from jax.experimental.pallas import tpu as pltpu
from jax.sharding import PartitionSpec as P

HEAD = 64
EPSILON = 1e-05
ROWS = 256
D = 1024
HALF = 512
OWNERS = 128
SLOTS = 4
HOPS = 4
LOG2E = 1.4426950408889634
SCALE = LOG2E * HEAD ** (-0.5)
MASKED = -1e30

bf16 = jnp.bfloat16
f32 = jnp.float32


def vmem():
    return pl.BlockSpec(memory_space=pltpu.VMEM)


def anywhere():
    return pl.BlockSpec(memory_space=pltpu.HBM)


def limit(mib):
    return pltpu.CompilerParams(vmem_limit_bytes=mib * 2**20)


def cost(flops, moved):
    return pl.CostEstimate(flops=flops, bytes_accessed=moved, transcendentals=0)


def slab_kernel(qkv, out, main, aux, half, keys, sems):
    par = lax.rem(lax.axis_index("seq"), 2)
    f = lax.axis_index("fsdp")
    copies = (
        pltpu.make_async_copy(qkv.at[:, pl.ds(pl.multiple_of(HALF * (par + f), HALF), HALF)], main, sems.at[0]),
        pltpu.make_async_copy(qkv.at[:, pl.ds(pl.multiple_of(D * (1 - f) + 256 * par, 256), 256)], aux, sems.at[1]),
        pltpu.make_async_copy(out.at[pl.ds(pl.multiple_of(HALF * par, HALF), HALF), :], half, sems.at[2]),
        pltpu.make_async_copy(qkv.at[:, pl.ds(pl.multiple_of(D * (1 - f), D), HALF)], keys, sems.at[3]),
    )
    for copy in copies:
        copy.start()
    for copy in copies:
        copy.wait()


def weight_kernel(keys, main, main_in, aux_in, aux_pair, wq, wk, wv):
    par = lax.rem(lax.axis_index("seq"), 2)
    f = lax.axis_index("fsdp")

    @pl.when(par == f)
    def _():
        wk[...] = keys[...]

    @pl.when(par != f)
    def _():
        wk[:, pl.ds(pl.multiple_of(par * 256, 256), 256)] = aux_in[...]
        wk[:, pl.ds(pl.multiple_of((1 - par) * 256, 256), 256)] = aux_pair[...]

    @pl.when(f == 0)
    def _():
        wq[...] = main[...]
        wv[...] = main_in[...]

    @pl.when(f == 1)
    def _():
        wq[...] = main_in[...]
        wv[...] = main[...]


def request_kernel(owner, rows, table, slot):
    orow = owner[...]
    above = lax.broadcasted_iota(jnp.int32, (ROWS, ROWS), 0)
    along = lax.broadcasted_iota(jnp.int32, (ROWS, ROWS), 1)
    ocol = jnp.sum(jnp.where(above == along, orow, 0), axis=1, keepdims=True)
    same = ocol == orow
    rank = jnp.sum(jnp.where(same & (above < along), 1, 0), axis=0, keepdims=True)
    rank_col = jnp.sum(jnp.where(same & (along < above), 1, 0), axis=1, keepdims=True)
    mine = lax.broadcasted_iota(jnp.int32, (OWNERS, ROWS), 0) == orow
    lane = lax.broadcasted_iota(jnp.int32, (OWNERS, 128), 1)
    out = jnp.zeros((OWNERS, 128), jnp.int32)
    for k in range(SLOTS):
        column = jnp.sum(jnp.where(mine & (rank == k), rows[...], 0), axis=1, keepdims=True)
        out = jnp.where(lane == k, column, out)
    table[...] = out
    slot[...] = ocol * SLOTS + rank_col


def norm_kernel(fetched, slot, dna, gain, normed, rim):
    pick = (lax.broadcasted_iota(jnp.int32, (ROWS, OWNERS * SLOTS), 1) == slot[...]).astype(f32).astype(bf16)
    site = jnp.dot(pick, fetched[...], preferred_element_type=f32)
    resid = dna[...].astype(f32) + site
    mean = jnp.mean(resid * resid, axis=1, keepdims=True)
    out = (resid * lax.rsqrt(mean + EPSILON) * gain[...]).astype(bf16)
    normed[...] = out
    rim[...] = out[ROWS - 8 :]


def conv_kernel(normed, rim, taps, out, padded):
    padded[pl.ds(0, 8), :] = rim[...].astype(f32)
    padded[pl.ds(8, ROWS), :] = normed[...].astype(f32)

    def column(c, carry):
        lanes = pl.ds(pl.multiple_of(c * 128, 128), 128)
        weight = taps[:, lanes].astype(f32)
        for part in range(2):
            total = jnp.zeros((128, 128), f32)
            for tap in range(7):
                total = total + weight[tap : tap + 1] * padded[pl.ds(part * 128 + 8 - tap, 128), lanes]
            out[pl.ds(part * 128, 128), lanes] = total.astype(bf16)
        return carry

    lax.fori_loop(0, D // 128, column, 0)


def q_kernel(own, other, wq, q):
    par = lax.rem(lax.axis_index("seq"), 2)
    for x, side in ((own, par), (other, 1 - par)):
        at = pl.ds(pl.multiple_of(side * ROWS, ROWS), ROWS)
        q[at, :] = jnp.dot(x[...], wq[...], preferred_element_type=f32).astype(bf16)


def blocks_of(k):
    if k == 0:
        return ((0, 0, 1), (1, 0, 0), (1, 1, 1))
    if k == HOPS:
        return ((0, 0, 2), (0, 1, 0), (1, 1, 2))
    return ((0, 0, 0), (0, 1, 0), (1, 0, 0), (1, 1, 0))


def score_block(k, own, other, wk, wv, q_ref, v_ref, e_ref, top_ref, sum_ref, k_ref):
    par = lax.rem(lax.axis_index("seq"), 2)
    for x, side in ((own, par), (other, 1 - par)):
        at = pl.ds(pl.multiple_of(side * ROWS, ROWS), ROWS)
        k_ref[at, :] = jnp.dot(x[...], wk[...], preferred_element_type=f32).astype(bf16)
        v_ref[at, :] = jnp.dot(x[...], wv[...], preferred_element_type=f32).astype(bf16)
    row = lax.broadcasted_iota(jnp.int32, (ROWS, ROWS), 0)
    col = lax.broadcasted_iota(jnp.int32, (ROWS, ROWS), 1)
    lane = lax.broadcasted_iota(jnp.int32, (ROWS, 128), 1)
    blocks = blocks_of(k)
    count = len(blocks)
    top_ref[...] = jnp.zeros((2, ROWS, 128), f32)
    sum_ref[...] = jnp.zeros((2, ROWS, 128), f32)

    def at_block(h, i):
        return pl.ds(pl.multiple_of((h * count + i) * ROWS, ROWS), ROWS)

    def pair(hp, carry):
        lanes = pl.ds(pl.multiple_of(hp * 128, 128), 128)
        tops = {}
        for side in range(2):
            h = 2 * hp + side
            for i, (qb, half, edge) in enumerate(blocks):
                q = q_ref[qb * ROWS : (qb + 1) * ROWS, lanes]
                q = jnp.where((lane < HEAD) == (side == 0), q, jnp.zeros_like(q))
                keys = k_ref[half * ROWS : (half + 1) * ROWS, lanes]
                s = lax.dot_general(q, keys, (((1,), (1,)), ((), ())), preferred_element_type=f32)
                if edge:
                    s = jnp.where(col <= row if edge == 1 else col > row, s, MASKED)
                e_ref[at_block(h, i), :] = s
                part = jnp.maximum(s[:, :128], s[:, 128:])
                known = tops.get((side, qb))
                tops[side, qb] = part if known is None else jnp.maximum(known, part)
        for side in range(2):
            h = 2 * hp + side
            for qb in range(2):
                top = jnp.max(tops[side, qb], axis=1, keepdims=True)
                total = None
                for i, (which, half, edge) in enumerate(blocks):
                    if which == qb:
                        e = jnp.exp2((e_ref[at_block(h, i), :] - top) * SCALE)
                        e_ref[at_block(h, i), :] = e
                        part = e[:, :128] + e[:, 128:]
                        total = part if total is None else total + part
                total = jnp.sum(total, axis=1, keepdims=True)
                top_ref[qb] = jnp.where(lane == h, top, top_ref[qb])
                sum_ref[qb] = jnp.where(lane == h, total, sum_ref[qb])
        return carry

    lax.fori_loop(0, 4, pair, 0)


def attend_kernel(*refs):
    q_ref, own, other, wk, wv = refs[:5]
    values, es, tops, sums = (refs[5 + HOPS * i : 5 + HOPS * (i + 1)] for i in range(4))
    mine, theirs, v_last, e_last, top_last, sum_last, k_last, factor, done = refs[5 + 4 * HOPS :]
    score_block(HOPS, own, other, wk, wv, q_ref, v_last, e_last, top_last, sum_last, k_last)
    values, es = values + (v_last,), es + (e_last,)
    tops, sums = tops + (top_last,), sums + (sum_last,)
    seq = lax.axis_index("seq")
    par = lax.rem(seq, 2)
    chip = seq // 2
    lane = lax.broadcasted_iota(jnp.int32, (ROWS, 128), 1)
    for qb in range(2):
        top = tops[0][qb]
        for k in range(1, HOPS + 1):
            top = jnp.where(chip >= k, jnp.maximum(top, tops[k][qb]), top)
        total = jnp.zeros((ROWS, 128), f32)
        for k in range(HOPS + 1):
            weight = jnp.exp2((tops[k][qb] - top) * SCALE)
            weight = jnp.where(chip >= k, weight, 0.0)
            factor[qb, k] = weight
            total = total + weight * sums[k][qb]
        inverse = 1.0 / jnp.where(lane < 8, total, 1.0)
        for k in range(HOPS + 1):
            factor[qb, k] = factor[qb, k] * inverse

    def pair(hp, carry):
        lanes = pl.ds(pl.multiple_of(hp * 128, 128), 128)
        for qb in range(2):
            outs = []
            for side in range(2):
                h = 2 * hp + side
                acc = None
                for k in range(HOPS + 1):
                    blocks = blocks_of(k)
                    column = jnp.sum(jnp.where(lane == h, factor[qb, k], 0.0), axis=1, keepdims=True)
                    for i, (which, half, edge) in enumerate(blocks):
                        if which == qb:
                            at = pl.ds(pl.multiple_of((h * len(blocks) + i) * ROWS, ROWS), ROWS)
                            p = (es[k][at, :] * column).astype(bf16)
                            value = values[k][half * ROWS : (half + 1) * ROWS, lanes]
                            part = jnp.dot(p, value, preferred_element_type=f32)
                            acc = part if acc is None else acc + part
                outs.append(acc)
            done[qb, :, lanes] = jnp.where(lane < HEAD, outs[0], outs[1])
        return carry

    lax.fori_loop(0, 4, pair, 0)
    mine[...] = done[par]
    theirs[...] = done[1 - par]


def out_kernel(mine, received, gain, w_here, w_mine, w_other, out):
    par = lax.rem(lax.axis_index("seq"), 2)
    f = lax.axis_index("fsdp")
    a, b = mine[...], received[...]
    mean = (jnp.sum(a * a, axis=1, keepdims=True) + jnp.sum(b * b, axis=1, keepdims=True)) / D
    scale = lax.rsqrt(mean + EPSILON)
    at_a = pl.ds(pl.multiple_of(par * HALF, HALF), HALF)
    at_b = pl.ds(pl.multiple_of((1 - par) * HALF, HALF), HALF)
    na = (a * scale * gain[:, at_a]).astype(bf16)
    nb = (b * scale * gain[:, at_b]).astype(bf16)
    here = jnp.dot(na, w_here[at_a, :], preferred_element_type=f32)
    here = here + jnp.dot(nb, w_here[at_b, :], preferred_element_type=f32)
    there = jnp.dot(na, w_mine[...], preferred_element_type=f32)
    there = there + jnp.dot(nb, w_other[...], preferred_element_type=f32)
    out[:, pl.ds(pl.multiple_of(f * HALF, HALF), HALF)] = here.astype(bf16)
    out[:, pl.ds(pl.multiple_of((1 - f) * HALF, HALF), HALF)] = there.astype(bf16)


def local(dna_embed, site_owner, site_row, variant_table, norm_gain, conv_weight, qkv_weight, out_weight, attn_gain):
    count = lax.axis_size("seq")
    across = [(0, 1), (1, 0)]
    swap = [(i, i ^ 1) for i in range(count)]
    ahead = [(i, i + 2) for i in range(count - 2)]

    main, aux, half, keys = pl.pallas_call(
        slab_kernel,
        out_shape=(
            jax.ShapeDtypeStruct((D, HALF), bf16),
            jax.ShapeDtypeStruct((D, 256), bf16),
            jax.ShapeDtypeStruct((HALF, HALF), bf16),
            jax.ShapeDtypeStruct((D, HALF), bf16),
        ),
        in_specs=[anywhere()] * 2,
        out_specs=(vmem(), vmem(), vmem(), vmem()),
        scratch_shapes=[pltpu.SemaphoreType.DMA((4,))],
        compiler_params=limit(6),
        name="slabs",
    )(*(pltpu.with_memory_space_constraint(w, pltpu.HBM) for w in (qkv_weight, out_weight)))
    main_in = lax.ppermute(main, "fsdp", across)
    aux_in = lax.ppermute(aux, "fsdp", across)
    out_in = lax.ppermute(half, "fsdp", across)
    aux_pair = lax.ppermute(aux_in, "seq", swap)
    out_pair = lax.ppermute(out_in, "seq", swap)

    table, slot = pl.pallas_call(
        request_kernel,
        out_shape=(jax.ShapeDtypeStruct((OWNERS, 128), jnp.int32), jax.ShapeDtypeStruct((ROWS, 1), jnp.int32)),
        in_specs=[vmem()] * 2,
        out_specs=(vmem(), vmem()),
        compiler_params=limit(4),
        name="requests",
    )(site_owner.reshape(1, ROWS), site_row)
    wanted = lax.all_to_all(table, "seq", split_axis=0, concat_axis=0, tiled=True)
    found = variant_table[wanted[:, :SLOTS].reshape(OWNERS * SLOTS)]
    fetched = lax.all_to_all(found, "seq", split_axis=0, concat_axis=0, tiled=True)
    normed, edge = pl.pallas_call(
        norm_kernel,
        out_shape=(jax.ShapeDtypeStruct((ROWS, D), bf16), jax.ShapeDtypeStruct((8, D), bf16)),
        in_specs=[vmem()] * 4,
        out_specs=(vmem(), vmem()),
        compiler_params=limit(10),
    name="norm",
    )(fetched, slot, dna_embed[0], norm_gain.reshape(1, D))
    rim = lax.ppermute(edge, "seq", [(i, i + 1) for i in range(count - 1)])
    x = pl.pallas_call(
        conv_kernel,
        out_shape=jax.ShapeDtypeStruct((ROWS, D), bf16),
        in_specs=[vmem()] * 3,
        out_specs=vmem(),
        scratch_shapes=[pltpu.VMEM((ROWS + 8, D), f32)],
        compiler_params=limit(6),
        name="conv",
    )(normed, rim, conv_weight)
    own = [x]
    for _ in range(HOPS):
        own.append(lax.ppermute(own[-1], "seq", ahead))
    other = []
    for hop in range(HOPS + 1):
        other.append(lax.ppermute(own[hop], "seq", swap))

    wq, wk, wv = pl.pallas_call(
        weight_kernel,
        out_shape=(jax.ShapeDtypeStruct((D, HALF), bf16),) * 3,
        in_specs=[vmem()] * 5,
        out_specs=(vmem(), vmem(), vmem()),
        compiler_params=limit(8),
        cost_estimate=cost(10**6, 6 * 2**20),
        name="weights",
    )(keys, main, main_in, aux_in, aux_pair)
    q = pl.pallas_call(
        q_kernel,
        out_shape=jax.ShapeDtypeStruct((2 * ROWS, HALF), bf16),
        in_specs=[vmem()] * 3,
        out_specs=vmem(),
        cost_estimate=cost(2 * 512 * D * HALF, 3 * 2**20),
        compiler_params=limit(6),
    name="queries",
    )(x, other[0], wq)

    def stats():
        return jax.ShapeDtypeStruct((2, ROWS, 128), f32)

    found = []
    for hop in range(HOPS):
        size = len(blocks_of(hop)) * 8 * ROWS
        found.append(
            pl.pallas_call(
                functools.partial(score_block, hop),
                out_shape=(
                    jax.ShapeDtypeStruct((2 * ROWS, HALF), bf16),
                    jax.ShapeDtypeStruct((size, ROWS), f32),
                    stats(),
                    stats(),
                ),
                in_specs=[vmem()] * 5,
                out_specs=(vmem(),) * 4,
                scratch_shapes=[pltpu.VMEM((2 * ROWS, HALF), bf16)],
                compiler_params=limit(4),
                cost_estimate=cost(2 * 10**9, 4 * 2**20),
                name="near",
            )(own[hop], other[hop], wk, wv, q)
        )
    mine, theirs = pl.pallas_call(
        attend_kernel,
        out_shape=(jax.ShapeDtypeStruct((ROWS, HALF), f32), jax.ShapeDtypeStruct((ROWS, HALF), f32)),
        in_specs=[vmem()] * (5 + 4 * HOPS),
        out_specs=(vmem(), vmem()),
        scratch_shapes=[
            pltpu.VMEM((2 * ROWS, HALF), bf16),
            pltpu.VMEM((len(blocks_of(HOPS)) * 8 * ROWS, ROWS), f32),
            pltpu.VMEM((2, ROWS, 128), f32),
            pltpu.VMEM((2, ROWS, 128), f32),
            pltpu.VMEM((2 * ROWS, HALF), bf16),
            pltpu.VMEM((2, HOPS + 1, ROWS, 128), f32),
            pltpu.VMEM((2, ROWS, HALF), f32),
        ],
        compiler_params=limit(14),
        cost_estimate=cost(5 * 10**9, 6 * 2**20),
        name="attend",
    )(q, own[HOPS], other[HOPS], wk, wv, *(found[k][i] for i in range(4) for k in range(HOPS)))
    received = lax.ppermute(theirs, "seq", swap)
    mixed = pl.pallas_call(
        out_kernel,
        out_shape=jax.ShapeDtypeStruct((ROWS, D), bf16),
        in_specs=[vmem()] * 6,
        out_specs=vmem(),
        compiler_params=limit(10),
        name="project",
    )(mine, received, attn_gain.reshape(1, D), out_weight, out_in, out_pair)
    return mixed[None]


def solution(mesh):
    in_specs = (
        P("fsdp", "seq", None),
        P("fsdp", "seq", None),
        P("fsdp", "seq"),
        P("seq", None),
        P(),
        P(),
        P(None, "fsdp"),
        P(None, "fsdp"),
        P(),
    )

    return jax.shard_map(local, mesh=mesh, in_specs=in_specs, out_specs=P("fsdp", "seq", None), check_vma=False)
```

```python
import functools

import jax
import jax.numpy as jnp
from jax import lax
from jax.experimental import pallas as pl
from jax.experimental.pallas import tpu as pltpu
from jax.sharding import PartitionSpec as P

HEAD = 64
EPSILON = 1e-05
ROWS = 256
D = 1024
HALF = 512
OWNERS = 128
SLOTS = 4
HOPS = 4
LOG2E = 1.4426950408889634
SCALE = LOG2E * HEAD ** (-0.5)
MASKED = -1e30

bf16 = jnp.bfloat16
f32 = jnp.float32


def vmem():
    return pl.BlockSpec(memory_space=pltpu.VMEM)


def anywhere():
    return pl.BlockSpec(memory_space=pltpu.HBM)


def limit(mib):
    return pltpu.CompilerParams(vmem_limit_bytes=mib * 2**20)


def cost(flops, moved):
    return pl.CostEstimate(flops=flops, bytes_accessed=moved, transcendentals=0)


def slab_kernel(qkv, out, main, aux, half, keys, sems):
    par = lax.rem(lax.axis_index("seq"), 2)
    f = lax.axis_index("fsdp")
    copies = (
        pltpu.make_async_copy(qkv.at[:, pl.ds(pl.multiple_of(HALF * (par + f), HALF), HALF)], main, sems.at[0]),
        pltpu.make_async_copy(qkv.at[:, pl.ds(pl.multiple_of(D * (1 - f) + 256 * par, 256), 256)], aux, sems.at[1]),
        pltpu.make_async_copy(out.at[pl.ds(pl.multiple_of(HALF * par, HALF), HALF), :], half, sems.at[2]),
        pltpu.make_async_copy(qkv.at[:, pl.ds(pl.multiple_of(D * (1 - f), D), HALF)], keys, sems.at[3]),
    )
    for copy in copies:
        copy.start()
    for copy in copies:
        copy.wait()


def weight_kernel(keys, main, main_in, aux_in, aux_pair, wq, wk, wv):
    par = lax.rem(lax.axis_index("seq"), 2)
    f = lax.axis_index("fsdp")

    @pl.when(par == f)
    def _():
        wk[...] = keys[...]

    @pl.when(par != f)
    def _():
        wk[:, pl.ds(pl.multiple_of(par * 256, 256), 256)] = aux_in[...]
        wk[:, pl.ds(pl.multiple_of((1 - par) * 256, 256), 256)] = aux_pair[...]

    @pl.when(f == 0)
    def _():
        wq[...] = main[...]
        wv[...] = main_in[...]

    @pl.when(f == 1)
    def _():
        wq[...] = main_in[...]
        wv[...] = main[...]


def request_kernel(owner, rows, table, slot):
    orow = owner[...]
    above = lax.broadcasted_iota(jnp.int32, (ROWS, ROWS), 0)
    along = lax.broadcasted_iota(jnp.int32, (ROWS, ROWS), 1)
    ocol = jnp.sum(jnp.where(above == along, orow, 0), axis=1, keepdims=True)
    same = ocol == orow
    rank = jnp.sum(jnp.where(same & (above < along), 1, 0), axis=0, keepdims=True)
    rank_col = jnp.sum(jnp.where(same & (along < above), 1, 0), axis=1, keepdims=True)
    mine = lax.broadcasted_iota(jnp.int32, (OWNERS, ROWS), 0) == orow
    lane = lax.broadcasted_iota(jnp.int32, (OWNERS, 128), 1)
    out = jnp.zeros((OWNERS, 128), jnp.int32)
    for k in range(SLOTS):
        column = jnp.sum(jnp.where(mine & (rank == k), rows[...], 0), axis=1, keepdims=True)
        out = jnp.where(lane == k, column, out)
    table[...] = out
    slot[...] = ocol * SLOTS + rank_col


def norm_kernel(fetched, slot, dna, gain, normed, rim, staged, sem):
    copy = pltpu.make_async_copy(dna, staged, sem)
    copy.start()
    pick = (lax.broadcasted_iota(jnp.int32, (ROWS, OWNERS * SLOTS), 1) == slot[...]).astype(f32).astype(bf16)
    site = jnp.dot(pick, fetched[...], preferred_element_type=f32)
    copy.wait()
    resid = staged[...].astype(f32) + site
    mean = jnp.mean(resid * resid, axis=1, keepdims=True)
    out = (resid * lax.rsqrt(mean + EPSILON) * gain[...]).astype(bf16)
    normed[...] = out
    rim[...] = out[ROWS - 8 :]


def conv_kernel(normed, rim, taps, out, padded):
    padded[pl.ds(0, 8), :] = rim[...].astype(f32)
    padded[pl.ds(8, ROWS), :] = normed[...].astype(f32)

    def column(c, carry):
        lanes = pl.ds(pl.multiple_of(c * 128, 128), 128)
        weight = taps[:, lanes].astype(f32)
        for part in range(2):
            total = jnp.zeros((128, 128), f32)
            for tap in range(7):
                total = total + weight[tap : tap + 1] * padded[pl.ds(part * 128 + 8 - tap, 128), lanes]
            out[pl.ds(part * 128, 128), lanes] = total.astype(bf16)
        return carry

    lax.fori_loop(0, D // 128, column, 0)


def q_kernel(own, other, wq, q):
    par = lax.rem(lax.axis_index("seq"), 2)
    for x, side in ((own, par), (other, 1 - par)):
        at = pl.ds(pl.multiple_of(side * ROWS, ROWS), ROWS)
        q[at, :] = jnp.dot(x[...], wq[...], preferred_element_type=f32).astype(bf16)


def blocks_of(k):
    if k == 0:
        return ((0, 0, 1), (1, 0, 0), (1, 1, 1))
    if k == HOPS:
        return ((0, 0, 2), (0, 1, 0), (1, 1, 2))
    return ((0, 0, 0), (0, 1, 0), (1, 0, 0), (1, 1, 0))


def score_block(k, own, other, wk, wv, q_ref, v_ref, e_ref, top_ref, sum_ref, k_ref, sc0, sc1):
    par = lax.rem(lax.axis_index("seq"), 2)
    for x, side in ((own, par), (other, 1 - par)):
        at = pl.ds(pl.multiple_of(side * ROWS, ROWS), ROWS)
        k_ref[at, :] = jnp.dot(x[...], wk[...], preferred_element_type=f32).astype(bf16)
        v_ref[at, :] = jnp.dot(x[...], wv[...], preferred_element_type=f32).astype(bf16)
    row = lax.broadcasted_iota(jnp.int32, (ROWS, ROWS), 0)
    col = lax.broadcasted_iota(jnp.int32, (ROWS, ROWS), 1)
    lane = lax.broadcasted_iota(jnp.int32, (ROWS, 128), 1)
    blocks = blocks_of(k)
    count = len(blocks)
    top_ref[...] = jnp.zeros((2, ROWS, 128), f32)
    sum_ref[...] = jnp.zeros((2, ROWS, 128), f32)

    def scores(hp, side, sc):
        lanes = pl.ds(pl.multiple_of(hp * 128, 128), 128)
        tops = [None, None]
        for i, (qb, half, edge) in enumerate(blocks):
            q = q_ref[qb * ROWS : (qb + 1) * ROWS, lanes]
            q = jnp.where((lane < HEAD) == (side == 0), q, jnp.zeros_like(q))
            keys = k_ref[half * ROWS : (half + 1) * ROWS, lanes]
            s = lax.dot_general(q, keys, (((1,), (1,)), ((), ())), preferred_element_type=f32)
            if edge:
                s = jnp.where(col <= row if edge == 1 else col > row, s, MASKED)
            sc[i] = s
            part = jnp.maximum(s[:, :128], s[:, 128:])
            tops[qb] = part if tops[qb] is None else jnp.maximum(tops[qb], part)
        return tuple(jnp.max(top, axis=1, keepdims=True) for top in tops)

    def weigh(h, sc, tops):
        for qb in range(2):
            total = None
            for i, (which, half, edge) in enumerate(blocks):
                if which == qb:
                    e = jnp.exp2((sc[i] - tops[qb]) * SCALE)
                    e_ref[pl.ds(pl.multiple_of((h * count + i) * ROWS, ROWS), ROWS), :] = e
                    part = e[:, :128] + e[:, 128:]
                    total = part if total is None else total + part
            total = jnp.sum(total, axis=1, keepdims=True)
            top_ref[qb] = jnp.where(lane == h, tops[qb], top_ref[qb])
            sum_ref[qb] = jnp.where(lane == h, total, sum_ref[qb])

    def pair(hp, even):
        odd = scores(hp, 1, sc1)
        weigh(2 * hp, sc0, even)
        after_it = scores(jnp.minimum(hp + 1, 3), 0, sc0)
        weigh(2 * hp + 1, sc1, odd)
        return after_it

    lax.fori_loop(0, 4, pair, scores(0, 0, sc0))


def attend_kernel(*refs):
    q_ref, own, other, wk, wv = refs[:5]
    values, es, tops, sums = (refs[5 + HOPS * i : 5 + HOPS * (i + 1)] for i in range(4))
    mine, theirs, v_last, e_last, top_last, sum_last, k_last, sc0, sc1, factor, done = refs[5 + 4 * HOPS :]
    score_block(HOPS, own, other, wk, wv, q_ref, v_last, e_last, top_last, sum_last, k_last, sc0, sc1)
    values, es = values + (v_last,), es + (e_last,)
    tops, sums = tops + (top_last,), sums + (sum_last,)
    seq = lax.axis_index("seq")
    par = lax.rem(seq, 2)
    chip = seq // 2
    lane = lax.broadcasted_iota(jnp.int32, (ROWS, 128), 1)
    for qb in range(2):
        top = tops[0][qb]
        for k in range(1, HOPS + 1):
            top = jnp.where(chip >= k, jnp.maximum(top, tops[k][qb]), top)
        total = jnp.zeros((ROWS, 128), f32)
        for k in range(HOPS + 1):
            weight = jnp.exp2((tops[k][qb] - top) * SCALE)
            weight = jnp.where(chip >= k, weight, 0.0)
            factor[qb, k] = weight
            total = total + weight * sums[k][qb]
        inverse = 1.0 / jnp.where(lane < 8, total, 1.0)
        for k in range(HOPS + 1):
            factor[qb, k] = factor[qb, k] * inverse

    def pair(hp, carry):
        lanes = pl.ds(pl.multiple_of(hp * 128, 128), 128)
        for qb in range(2):
            outs = []
            for side in range(2):
                h = 2 * hp + side
                acc = None
                for k in range(HOPS + 1):
                    blocks = blocks_of(k)
                    column = jnp.sum(jnp.where(lane == h, factor[qb, k], 0.0), axis=1, keepdims=True)
                    for i, (which, half, edge) in enumerate(blocks):
                        if which == qb:
                            at = pl.ds(pl.multiple_of((h * len(blocks) + i) * ROWS, ROWS), ROWS)
                            p = (es[k][at, :] * column).astype(bf16)
                            value = values[k][half * ROWS : (half + 1) * ROWS, lanes]
                            part = jnp.dot(p, value, preferred_element_type=f32)
                            acc = part if acc is None else acc + part
                outs.append(acc)
            done[qb, :, lanes] = jnp.where(lane < HEAD, outs[0], outs[1])
        return carry

    lax.fori_loop(0, 4, pair, 0)
    mine[...] = done[par]
    theirs[...] = done[1 - par]


def out_kernel(mine, received, gain, w_here, w_mine, w_other, out):
    par = lax.rem(lax.axis_index("seq"), 2)
    f = lax.axis_index("fsdp")
    a, b = mine[...], received[...]
    mean = (jnp.sum(a * a, axis=1, keepdims=True) + jnp.sum(b * b, axis=1, keepdims=True)) / D
    scale = lax.rsqrt(mean + EPSILON)
    at_a = pl.ds(pl.multiple_of(par * HALF, HALF), HALF)
    at_b = pl.ds(pl.multiple_of((1 - par) * HALF, HALF), HALF)
    na = (a * scale * gain[:, at_a]).astype(bf16)
    nb = (b * scale * gain[:, at_b]).astype(bf16)
    here = jnp.dot(na, w_here[at_a, :], preferred_element_type=f32)
    here = here + jnp.dot(nb, w_here[at_b, :], preferred_element_type=f32)
    there = jnp.dot(na, w_mine[...], preferred_element_type=f32)
    there = there + jnp.dot(nb, w_other[...], preferred_element_type=f32)
    out[:, pl.ds(pl.multiple_of(f * HALF, HALF), HALF)] = here.astype(bf16)
    out[:, pl.ds(pl.multiple_of((1 - f) * HALF, HALF), HALF)] = there.astype(bf16)


def local(dna_embed, site_owner, site_row, variant_table, norm_gain, conv_weight, qkv_weight, out_weight, attn_gain):
    count = lax.axis_size("seq")
    across = [(0, 1), (1, 0)]
    beyond = [(i, i ^ (count + 1)) for i in range(2 * count)]
    swap = [(i, i ^ 1) for i in range(count)]
    ahead = [(i, i + 2) for i in range(count - 2)]

    main, aux, half, keys = pl.pallas_call(
        slab_kernel,
        out_shape=(
            jax.ShapeDtypeStruct((D, HALF), bf16),
            jax.ShapeDtypeStruct((D, 256), bf16),
            jax.ShapeDtypeStruct((HALF, HALF), bf16),
            jax.ShapeDtypeStruct((D, HALF), bf16),
        ),
        in_specs=[anywhere()] * 2,
        out_specs=(vmem(),) * 4,
        scratch_shapes=[pltpu.SemaphoreType.DMA((4,))],
        compiler_params=limit(6),
        name="slabs",
    )(*(pltpu.with_memory_space_constraint(w, pltpu.HBM) for w in (qkv_weight, out_weight)))
    main_in = lax.ppermute(main, "fsdp", across)
    aux_in = lax.ppermute(aux, ("seq", "fsdp"), beyond)
    out_in = lax.ppermute(half, ("seq", "fsdp"), beyond)
    aux_pair = lax.ppermute(aux_in, "seq", swap)
    out_pair = lax.ppermute(out_in, "seq", swap)

    table, slot = pl.pallas_call(
        request_kernel,
        out_shape=(jax.ShapeDtypeStruct((OWNERS, 128), jnp.int32), jax.ShapeDtypeStruct((ROWS, 1), jnp.int32)),
        in_specs=[vmem()] * 2,
        out_specs=(vmem(), vmem()),
        compiler_params=limit(4),
        name="requests",
    )(site_owner.reshape(1, ROWS), site_row)
    wanted = lax.all_to_all(table, "seq", split_axis=0, concat_axis=0, tiled=True)
    found = variant_table[wanted[:, :SLOTS].reshape(OWNERS * SLOTS)]
    fetched = lax.all_to_all(found, "seq", split_axis=0, concat_axis=0, tiled=True)
    normed, edge = pl.pallas_call(
        norm_kernel,
        out_shape=(jax.ShapeDtypeStruct((ROWS, D), bf16), jax.ShapeDtypeStruct((8, D), bf16)),
        in_specs=[vmem(), vmem(), anywhere(), vmem()],
        out_specs=(vmem(), vmem()),
        scratch_shapes=[pltpu.VMEM((ROWS, D), bf16), pltpu.SemaphoreType.DMA],
        compiler_params=limit(10),
    name="norm",
    )(fetched, slot, pltpu.with_memory_space_constraint(dna_embed[0], pltpu.HBM), norm_gain.reshape(1, D))
    rim = lax.ppermute(edge, "seq", [(i, i + 1) for i in range(count - 1)])
    x = pl.pallas_call(
        conv_kernel,
        out_shape=jax.ShapeDtypeStruct((ROWS, D), bf16),
        in_specs=[vmem()] * 3,
        out_specs=vmem(),
        scratch_shapes=[pltpu.VMEM((ROWS + 8, D), f32)],
        compiler_params=limit(6),
        name="conv",
    )(normed, rim, conv_weight)
    own = [x]
    for _ in range(HOPS):
        own.append(lax.ppermute(own[-1], "seq", ahead))
    other = []
    for hop in range(HOPS + 1):
        other.append(lax.ppermute(own[hop], "seq", swap))

    wq, wk, wv = pl.pallas_call(
        weight_kernel,
        out_shape=(jax.ShapeDtypeStruct((D, HALF), bf16),) * 3,
        in_specs=[vmem()] * 5,
        out_specs=(vmem(), vmem(), vmem()),
        compiler_params=limit(8),
        cost_estimate=cost(10**6, 6 * 2**20),
        name="weights",
    )(keys, main, main_in, aux_in, aux_pair)
    q = pl.pallas_call(
        q_kernel,
        out_shape=jax.ShapeDtypeStruct((2 * ROWS, HALF), bf16),
        in_specs=[vmem()] * 3,
        out_specs=vmem(),
        cost_estimate=cost(2 * 512 * D * HALF, 3 * 2**20),
        compiler_params=limit(6),
    name="queries",
    )(x, other[0], wq)

    def stats():
        return jax.ShapeDtypeStruct((2, ROWS, 128), f32)

    found = []
    for hop in range(HOPS):
        size = len(blocks_of(hop)) * 8 * ROWS
        found.append(
            pl.pallas_call(
                functools.partial(score_block, hop),
                out_shape=(
                    jax.ShapeDtypeStruct((2 * ROWS, HALF), bf16),
                    jax.ShapeDtypeStruct((size, ROWS), f32),
                    stats(),
                    stats(),
                ),
                in_specs=[vmem()] * 5,
                out_specs=(vmem(),) * 4,
                scratch_shapes=[pltpu.VMEM((2 * ROWS, HALF), bf16)] + [pltpu.VMEM((4, ROWS, ROWS), f32)] * 2,
                compiler_params=limit(5),
                cost_estimate=cost(2 * 10**9, 4 * 2**20),
                name="near",
            )(own[hop], other[hop], wk, wv, q)
        )
    mine, theirs = pl.pallas_call(
        attend_kernel,
        out_shape=(jax.ShapeDtypeStruct((ROWS, HALF), f32), jax.ShapeDtypeStruct((ROWS, HALF), f32)),
        in_specs=[vmem()] * (5 + 4 * HOPS),
        out_specs=(vmem(), vmem()),
        scratch_shapes=[
            pltpu.VMEM((2 * ROWS, HALF), bf16),
            pltpu.VMEM((len(blocks_of(HOPS)) * 8 * ROWS, ROWS), f32),
            pltpu.VMEM((2, ROWS, 128), f32),
            pltpu.VMEM((2, ROWS, 128), f32),
            pltpu.VMEM((2 * ROWS, HALF), bf16),
            pltpu.VMEM((4, ROWS, ROWS), f32),
            pltpu.VMEM((4, ROWS, ROWS), f32),
            pltpu.VMEM((2, HOPS + 1, ROWS, 128), f32),
            pltpu.VMEM((2, ROWS, HALF), f32),
        ],
        compiler_params=limit(15),
        cost_estimate=cost(5 * 10**9, 6 * 2**20),
        name="attend",
    )(q, own[HOPS], other[HOPS], wk, wv, *(found[k][i] for i in range(4) for k in range(HOPS)))
    received = lax.ppermute(theirs, "seq", swap)
    mixed = pl.pallas_call(
        out_kernel,
        out_shape=jax.ShapeDtypeStruct((ROWS, D), bf16),
        in_specs=[vmem()] * 6,
        out_specs=vmem(),
        compiler_params=limit(10),
        name="project",
    )(mine, received, attn_gain.reshape(1, D), out_weight, out_in, out_pair)
    return mixed[None]


def solution(mesh):
    in_specs = (
        P("fsdp", "seq", None),
        P("fsdp", "seq", None),
        P("fsdp", "seq"),
        P("seq", None),
        P(),
        P(),
        P(None, "fsdp"),
        P(None, "fsdp"),
        P(),
    )

    return jax.shard_map(local, mesh=mesh, in_specs=in_specs, out_specs=P("fsdp", "seq", None), check_vma=False)
```

```python
import functools

import jax
import jax.numpy as jnp
from jax import lax
from jax.experimental import pallas as pl
from jax.experimental.pallas import tpu as pltpu
from jax.sharding import PartitionSpec as P

HEAD = 64
EPSILON = 1e-05
ROWS = 256
D = 1024
HALF = 512
OWNERS = 128
SLOTS = 4
HOPS = 4
Z = 8
LOG2E = 1.4426950408889634
SCALE = LOG2E * HEAD ** (-0.5)
MASKED = -1e30

bf16 = jnp.bfloat16
f32 = jnp.float32


def vmem():
    return pl.BlockSpec(memory_space=pltpu.VMEM)


def anywhere():
    return pl.BlockSpec(memory_space=pltpu.HBM)


def limit(mib):
    return pltpu.CompilerParams(vmem_limit_bytes=mib * 2**20)


def cost(flops, moved):
    return pl.CostEstimate(flops=flops, bytes_accessed=moved, transcendentals=0)


def slab_kernel(qkv, out, main, aux, half, keys, sems):
    par = lax.rem(lax.axis_index("seq"), 2)
    f = lax.axis_index("fsdp")
    copies = (
        pltpu.make_async_copy(qkv.at[:, pl.ds(pl.multiple_of(HALF * (par + f), HALF), HALF)], main, sems.at[0]),
        pltpu.make_async_copy(qkv.at[:, pl.ds(pl.multiple_of(D * (1 - f) + 256 * par, 256), 256)], aux, sems.at[1]),
        pltpu.make_async_copy(out.at[pl.ds(pl.multiple_of(HALF * par, HALF), HALF), :], half, sems.at[2]),
        pltpu.make_async_copy(qkv.at[:, pl.ds(pl.multiple_of(D * (1 - f), D), HALF)], keys, sems.at[3]),
    )
    for copy in copies:
        copy.start()
    for copy in copies:
        copy.wait()


def weight_kernel(keys, main, main_in, aux_in, aux_pair, wq, wk, wv):
    par = lax.rem(lax.axis_index("seq"), 2)
    f = lax.axis_index("fsdp")

    @pl.when(par == f)
    def _():
        wk[...] = keys[...]

    @pl.when(par != f)
    def _():
        wk[:, pl.ds(pl.multiple_of(par * 256, 256), 256)] = aux_in[...]
        wk[:, pl.ds(pl.multiple_of((1 - par) * 256, 256), 256)] = aux_pair[...]

    @pl.when(f == 0)
    def _():
        wq[...] = main[...]
        wv[...] = main_in[...]

    @pl.when(f == 1)
    def _():
        wq[...] = main_in[...]
        wv[...] = main[...]


def request_kernel(owner, rows_in, table, slot, owners, rows, sems):
    first = pltpu.make_async_copy(owner, owners, sems.at[0])
    second = pltpu.make_async_copy(rows_in, rows, sems.at[1])
    first.start()
    second.start()
    first.wait()
    second.wait()
    orow = owners[...]
    above = lax.broadcasted_iota(jnp.int32, (ROWS, ROWS), 0)
    along = lax.broadcasted_iota(jnp.int32, (ROWS, ROWS), 1)
    ocol = jnp.sum(jnp.where(above == along, orow, 0), axis=1, keepdims=True)
    same = ocol == orow
    rank = jnp.sum(jnp.where(same & (above < along), 1, 0), axis=0, keepdims=True)
    rank_col = jnp.sum(jnp.where(same & (along < above), 1, 0), axis=1, keepdims=True)
    mine = lax.broadcasted_iota(jnp.int32, (OWNERS, ROWS), 0) == orow
    lane = lax.broadcasted_iota(jnp.int32, (OWNERS, 128), 1)
    out = jnp.zeros((OWNERS, 128), jnp.int32)
    for k in range(SLOTS):
        column = jnp.sum(jnp.where(mine & (rank == k), rows[...], 0), axis=1, keepdims=True)
        out = jnp.where(lane == k, column, out)
    table[...] = out
    slot[...] = ocol * SLOTS + rank_col


def norm_kernel(fetched, slot, dna, gain, normed, rim, staged, sem):
    copy = pltpu.make_async_copy(dna, staged, sem)
    copy.start()
    pick = (lax.broadcasted_iota(jnp.int32, (ROWS, OWNERS * SLOTS), 1) == slot[...]).astype(f32).astype(bf16)
    site = jnp.dot(pick, fetched[...], preferred_element_type=f32)
    copy.wait()
    resid = staged[...].astype(f32) + site
    mean = jnp.mean(resid * resid, axis=1, keepdims=True)
    out = (resid * lax.rsqrt(mean + EPSILON) * gain[...]).astype(bf16)
    normed[...] = out
    rim[...] = out[ROWS - 8 :]


def conv_kernel(normed, rim, taps, out, padded):
    padded[pl.ds(0, 8), :] = rim[...].astype(f32)
    padded[pl.ds(8, ROWS), :] = normed[...].astype(f32)

    def column(c, carry):
        lanes = pl.ds(pl.multiple_of(c * 128, 128), 128)
        weight = taps[:, lanes].astype(f32)
        for part in range(2):
            total = jnp.zeros((128, 128), f32)
            for tap in range(7):
                total = total + weight[tap : tap + 1] * padded[pl.ds(part * 128 + 8 - tap, 128), lanes]
            out[pl.ds(part * 128, 128), lanes] = total.astype(bf16)
        return carry

    lax.fori_loop(0, D // 128, column, 0)


def q_kernel(own, other, wq, q):
    par = lax.rem(lax.axis_index("seq"), 2)
    for x, side in ((own, par), (other, 1 - par)):
        at = pl.ds(pl.multiple_of(side * ROWS, ROWS), ROWS)
        q[at, :] = jnp.dot(x[...], wq[...], preferred_element_type=f32).astype(bf16)


def blocks_of(k):
    if k == 0:
        return ((0, 0, 1), (1, 0, 0), (1, 1, 1))
    if k == HOPS:
        return ((0, 0, 2), (0, 1, 0), (1, 1, 2))
    return ((0, 0, 0), (0, 1, 0), (1, 0, 0), (1, 1, 0))


def score_block(k, own, other, wk, wv, q_ref, v_ref, e_ref, top_ref, sum_ref, k_ref, sc0, sc1):
    par = lax.rem(lax.axis_index("seq"), 2)
    for x, side in ((own, par), (other, 1 - par)):
        at = pl.ds(pl.multiple_of(side * ROWS, ROWS), ROWS)
        k_ref[at, :] = jnp.dot(x[...], wk[...], preferred_element_type=f32).astype(bf16)
        v_ref[at, :] = jnp.dot(x[...], wv[...], preferred_element_type=f32).astype(bf16)
    row = lax.broadcasted_iota(jnp.int32, (ROWS, ROWS), 0)
    col = lax.broadcasted_iota(jnp.int32, (ROWS, ROWS), 1)
    lane = lax.broadcasted_iota(jnp.int32, (ROWS, 128), 1)
    blocks = blocks_of(k)
    count = len(blocks)
    top_ref[...] = jnp.zeros((2, ROWS, 128), f32)
    sum_ref[...] = jnp.zeros((2, ROWS, 128), f32)

    def scores(hp, side, sc):
        lanes = pl.ds(pl.multiple_of(hp * 128, 128), 128)
        tops = [None, None]
        for i, (qb, half, edge) in enumerate(blocks):
            q = q_ref[qb * ROWS : (qb + 1) * ROWS, lanes]
            q = jnp.where((lane < HEAD) == (side == 0), q, jnp.zeros_like(q))
            keys = k_ref[half * ROWS : (half + 1) * ROWS, lanes]
            s = lax.dot_general(q, keys, (((1,), (1,)), ((), ())), preferred_element_type=f32)
            if edge:
                s = jnp.where(col <= row if edge == 1 else col > row, s, MASKED)
            sc[i] = s
            part = jnp.maximum(s[:, :128], s[:, 128:])
            tops[qb] = part if tops[qb] is None else jnp.maximum(tops[qb], part)
        return tuple(jnp.max(top, axis=1, keepdims=True) for top in tops)

    def weigh(h, sc, tops):
        for qb in range(2):
            total = None
            for i, (which, half, edge) in enumerate(blocks):
                if which == qb:
                    e = jnp.exp2((sc[i] - tops[qb]) * SCALE)
                    e_ref[pl.ds(pl.multiple_of((h * count + i) * ROWS, ROWS), ROWS), :] = e
                    part = e[:, :128] + e[:, 128:]
                    total = part if total is None else total + part
            total = jnp.sum(total, axis=1, keepdims=True)
            top_ref[qb] = jnp.where(lane == h, tops[qb], top_ref[qb])
            sum_ref[qb] = jnp.where(lane == h, total, sum_ref[qb])

    def pair(hp, even):
        odd = scores(hp, 1, sc1)
        weigh(2 * hp, sc0, even)
        after_it = scores(jnp.minimum(hp + 1, 3), 0, sc0)
        weigh(2 * hp + 1, sc1, odd)
        return after_it

    lax.fori_loop(0, 4, pair, scores(0, 0, sc0))


def attend_kernel(*refs):
    q_ref, own, other, wk, wv = refs[:5]
    values, es, tops, sums = (refs[5 + HOPS * i : 5 + HOPS * (i + 1)] for i in range(4))
    mine, theirs, v_last, e_last, top_last, sum_last, k_last, sc0, sc1, factor, done = refs[5 + 4 * HOPS :]
    score_block(HOPS, own, other, wk, wv, q_ref, v_last, e_last, top_last, sum_last, k_last, sc0, sc1)
    values, es = values + (v_last,), es + (e_last,)
    tops, sums = tops + (top_last,), sums + (sum_last,)
    seq = lax.axis_index("seq")
    par = lax.rem(seq, 2)
    chip = seq // 2
    lane = lax.broadcasted_iota(jnp.int32, (ROWS, 128), 1)
    for qb in range(2):
        top = tops[0][qb]
        for k in range(1, HOPS + 1):
            top = jnp.where(chip >= k, jnp.maximum(top, tops[k][qb]), top)
        total = jnp.zeros((ROWS, 128), f32)
        for k in range(HOPS + 1):
            weight = jnp.exp2((tops[k][qb] - top) * SCALE)
            weight = jnp.where(chip >= k, weight, 0.0)
            factor[qb, k] = weight
            total = total + weight * sums[k][qb]
        inverse = 1.0 / jnp.where(lane < 8, total, 1.0)
        for k in range(HOPS + 1):
            factor[qb, k] = factor[qb, k] * inverse

    def pair(hp, carry):
        lanes = pl.ds(pl.multiple_of(hp * 128, 128), 128)
        for qb in range(2):
            outs = []
            for side in range(2):
                h = 2 * hp + side
                acc = None
                for k in range(HOPS + 1):
                    blocks = blocks_of(k)
                    column = jnp.sum(jnp.where(lane == h, factor[qb, k], 0.0), axis=1, keepdims=True)
                    for i, (which, half, edge) in enumerate(blocks):
                        if which == qb:
                            at = pl.ds(pl.multiple_of((h * len(blocks) + i) * ROWS, ROWS), ROWS)
                            p = (es[k][at, :] * column).astype(bf16)
                            value = values[k][half * ROWS : (half + 1) * ROWS, lanes]
                            part = jnp.dot(p, value, preferred_element_type=f32)
                            acc = part if acc is None else acc + part
                outs.append(acc)
            done[qb, :, lanes] = jnp.where(lane < HEAD, outs[0], outs[1])
        return carry

    lax.fori_loop(0, 4, pair, 0)
    mine[...] = done[par]
    theirs[...] = done[1 - par]


def out_kernel(mine, received, gain, w_here, w_mine, w_other, out):
    par = lax.rem(lax.axis_index("seq"), 2)
    f = lax.axis_index("fsdp")
    a, b = mine[...], received[...]
    mean = (jnp.sum(a * a, axis=1, keepdims=True) + jnp.sum(b * b, axis=1, keepdims=True)) / D
    scale = lax.rsqrt(mean + EPSILON)
    at_a = pl.ds(pl.multiple_of(par * HALF, HALF), HALF)
    at_b = pl.ds(pl.multiple_of((1 - par) * HALF, HALF), HALF)
    na = (a * scale * gain[:, at_a]).astype(bf16)
    nb = (b * scale * gain[:, at_b]).astype(bf16)
    here = jnp.dot(na, w_here[at_a, :], preferred_element_type=f32)
    here = here + jnp.dot(nb, w_here[at_b, :], preferred_element_type=f32)
    there = jnp.dot(na, w_mine[...], preferred_element_type=f32)
    there = there + jnp.dot(nb, w_other[...], preferred_element_type=f32)
    out[:, pl.ds(pl.multiple_of(f * HALF, HALF), HALF)] = here.astype(bf16)
    out[:, pl.ds(pl.multiple_of((1 - f) * HALF, HALF), HALF)] = there.astype(bf16)


def local(dna_embed, site_owner, site_row, variant_table, norm_gain, conv_weight, qkv_weight, out_weight, attn_gain):
    count = lax.axis_size("seq")
    across = [(0, 1), (1, 0)]
    beyond = [(i, i ^ (count + 1)) for i in range(2 * count)]
    swap = [(i, i ^ 1) for i in range(count)]
    ahead = [(i, i + 2) for i in range(count - 2)]

    main, aux, half, keys = pl.pallas_call(
        slab_kernel,
        out_shape=(
            jax.ShapeDtypeStruct((D, HALF), bf16),
            jax.ShapeDtypeStruct((D, 256), bf16),
            jax.ShapeDtypeStruct((HALF, HALF), bf16),
            jax.ShapeDtypeStruct((D, HALF), bf16),
        ),
        in_specs=[anywhere()] * 2,
        out_specs=(vmem(),) * 4,
        scratch_shapes=[pltpu.SemaphoreType.DMA((4,))],
        compiler_params=limit(6),
        name="slabs",
    )(*(pltpu.with_memory_space_constraint(w, pltpu.HBM) for w in (qkv_weight, out_weight)))
    main_in = lax.ppermute(main, "fsdp", across)
    aux_in = lax.ppermute(aux, ("seq", "fsdp"), beyond)
    out_in = lax.ppermute(half, ("seq", "fsdp"), beyond)
    aux_pair = lax.ppermute(aux_in, "seq", swap)
    out_pair = lax.ppermute(out_in, "seq", swap)

    table, slot = pl.pallas_call(
        request_kernel,
        out_shape=(jax.ShapeDtypeStruct((OWNERS, 128), jnp.int32), jax.ShapeDtypeStruct((ROWS, 1), jnp.int32)),
        in_specs=[anywhere()] * 2,
        out_specs=(vmem(), vmem()),
        scratch_shapes=[pltpu.VMEM((1, ROWS), jnp.int32)] * 2 + [pltpu.SemaphoreType.DMA((2,))],
        compiler_params=limit(4),
        name="requests",
    )(*(pltpu.with_memory_space_constraint(v, pltpu.HBM) for v in (site_owner.reshape(1, ROWS), site_row)))
    wanted = lax.all_to_all(table, "seq", split_axis=0, concat_axis=0, tiled=True)
    found = variant_table[wanted[:, :SLOTS].reshape(OWNERS * SLOTS)]
    fetched = lax.all_to_all(found, "seq", split_axis=0, concat_axis=0, tiled=True)
    normed, edge = pl.pallas_call(
        norm_kernel,
        out_shape=(jax.ShapeDtypeStruct((ROWS, D), bf16), jax.ShapeDtypeStruct((8, D), bf16)),
        in_specs=[vmem(), vmem(), anywhere(), vmem()],
        out_specs=(vmem(), vmem()),
        scratch_shapes=[pltpu.VMEM((ROWS, D), bf16), pltpu.SemaphoreType.DMA],
        compiler_params=limit(10),
    name="norm",
    )(fetched, slot, pltpu.with_memory_space_constraint(dna_embed[0], pltpu.HBM), norm_gain.reshape(1, D))
    rim = lax.ppermute(edge, "seq", [(i, i + 1) for i in range(count - 1)])
    x = pl.pallas_call(
        conv_kernel,
        out_shape=jax.ShapeDtypeStruct((ROWS, D), bf16),
        in_specs=[vmem()] * 3,
        out_specs=vmem(),
        scratch_shapes=[pltpu.VMEM((ROWS + 8, D), f32)],
        compiler_params=limit(6),
        name="conv",
    )(normed, rim, conv_weight)
    own = [x]
    for _ in range(HOPS - 1):
        own.append(lax.ppermute(own[-1], "seq", ahead))
    ring, reach = 2 * Z, 2 * HOPS
    behind = [i // ring * ring + (i - 6) % ring for i in range(count - reach)]
    far = lax.ppermute(x, "seq", list(enumerate(behind)))
    own.append(lax.ppermute(far, "seq", [(b, i + reach) for i, b in enumerate(behind)]))
    other = []
    for hop in range(HOPS + 1):
        other.append(lax.ppermute(own[hop], "seq", swap))

    wq, wk, wv = pl.pallas_call(
        weight_kernel,
        out_shape=(jax.ShapeDtypeStruct((D, HALF), bf16),) * 3,
        in_specs=[vmem()] * 5,
        out_specs=(vmem(), vmem(), vmem()),
        compiler_params=limit(8),
        cost_estimate=cost(10**6, 6 * 2**20),
        name="weights",
    )(keys, main, main_in, aux_in, aux_pair)
    q = pl.pallas_call(
        q_kernel,
        out_shape=jax.ShapeDtypeStruct((2 * ROWS, HALF), bf16),
        in_specs=[vmem()] * 3,
        out_specs=vmem(),
        cost_estimate=cost(2 * 512 * D * HALF, 3 * 2**20),
        compiler_params=limit(6),
    name="queries",
    )(x, other[0], wq)

    def stats():
        return jax.ShapeDtypeStruct((2, ROWS, 128), f32)

    found = []
    for hop in range(HOPS):
        size = len(blocks_of(hop)) * 8 * ROWS
        found.append(
            pl.pallas_call(
                functools.partial(score_block, hop),
                out_shape=(
                    jax.ShapeDtypeStruct((2 * ROWS, HALF), bf16),
                    jax.ShapeDtypeStruct((size, ROWS), f32),
                    stats(),
                    stats(),
                ),
                in_specs=[vmem()] * 5,
                out_specs=(vmem(),) * 4,
                scratch_shapes=[pltpu.VMEM((2 * ROWS, HALF), bf16)] + [pltpu.VMEM((4, ROWS, ROWS), f32)] * 2,
                compiler_params=limit(5),
                cost_estimate=cost(2 * 10**9, 4 * 2**20),
                name="near",
            )(own[hop], other[hop], wk, wv, q)
        )
    mine, theirs = pl.pallas_call(
        attend_kernel,
        out_shape=(jax.ShapeDtypeStruct((ROWS, HALF), f32), jax.ShapeDtypeStruct((ROWS, HALF), f32)),
        in_specs=[vmem()] * (5 + 4 * HOPS),
        out_specs=(vmem(), vmem()),
        scratch_shapes=[
            pltpu.VMEM((2 * ROWS, HALF), bf16),
            pltpu.VMEM((len(blocks_of(HOPS)) * 8 * ROWS, ROWS), f32),
            pltpu.VMEM((2, ROWS, 128), f32),
            pltpu.VMEM((2, ROWS, 128), f32),
            pltpu.VMEM((2 * ROWS, HALF), bf16),
            pltpu.VMEM((4, ROWS, ROWS), f32),
            pltpu.VMEM((4, ROWS, ROWS), f32),
            pltpu.VMEM((2, HOPS + 1, ROWS, 128), f32),
            pltpu.VMEM((2, ROWS, HALF), f32),
        ],
        compiler_params=limit(15),
        cost_estimate=cost(5 * 10**9, 6 * 2**20),
        name="attend",
    )(q, own[HOPS], other[HOPS], wk, wv, *(found[k][i] for i in range(4) for k in range(HOPS)))
    received = lax.ppermute(theirs, "seq", swap)
    mixed = pl.pallas_call(
        out_kernel,
        out_shape=jax.ShapeDtypeStruct((ROWS, D), bf16),
        in_specs=[vmem()] * 6,
        out_specs=vmem(),
        compiler_params=limit(10),
        name="project",
    )(mine, received, attn_gain.reshape(1, D), out_weight, out_in, out_pair)
    return mixed[None]


def solution(mesh):
    in_specs = (
        P("fsdp", "seq", None),
        P("fsdp", "seq", None),
        P("fsdp", "seq"),
        P("seq", None),
        P(),
        P(),
        P(None, "fsdp"),
        P(None, "fsdp"),
        P(),
    )

    return jax.shard_map(local, mesh=mesh, in_specs=in_specs, out_specs=P("fsdp", "seq", None), check_vma=False)
```

```python
import functools

import jax
import jax.numpy as jnp
from jax import lax
from jax.experimental import pallas as pl
from jax.experimental.pallas import tpu as pltpu
from jax.sharding import PartitionSpec as P

HEAD = 64
EPSILON = 1e-05
ROWS = 256
D = 1024
HALF = 512
OWNERS = 128
SLOTS = 4
HOPS = 4
Z = 8
LOG2E = 1.4426950408889634
SCALE = LOG2E * HEAD ** (-0.5)
MASKED = -1e30

bf16 = jnp.bfloat16
f32 = jnp.float32


def vmem():
    return pl.BlockSpec(memory_space=pltpu.VMEM)


def anywhere():
    return pl.BlockSpec(memory_space=pltpu.HBM)


def limit(mib):
    return pltpu.CompilerParams(vmem_limit_bytes=mib * 2**20)


def cost(flops, moved):
    return pl.CostEstimate(flops=flops, bytes_accessed=moved, transcendentals=0)


def slab_kernel(qkv, out, main, aux, half, keys, sems):
    par = lax.rem(lax.axis_index("seq"), 2)
    f = lax.axis_index("fsdp")
    copies = (
        pltpu.make_async_copy(qkv.at[:, pl.ds(pl.multiple_of(HALF * (par + f), HALF), HALF)], main, sems.at[0]),
        pltpu.make_async_copy(qkv.at[:, pl.ds(pl.multiple_of(D * (1 - f) + 256 * par, 256), 256)], aux, sems.at[1]),
        pltpu.make_async_copy(out.at[pl.ds(pl.multiple_of(HALF * par, HALF), HALF), :], half, sems.at[2]),
        pltpu.make_async_copy(qkv.at[:, pl.ds(pl.multiple_of(D * (1 - f), D), HALF)], keys, sems.at[3]),
    )
    for copy in copies:
        copy.start()
    for copy in copies:
        copy.wait()


def weight_kernel(keys, main, main_in, aux_in, aux_pair, wq, wk, wv):
    par = lax.rem(lax.axis_index("seq"), 2)
    f = lax.axis_index("fsdp")

    @pl.when(par == f)
    def _():
        wk[...] = keys[...]

    @pl.when(par != f)
    def _():
        wk[:, pl.ds(pl.multiple_of(par * 256, 256), 256)] = aux_in[...]
        wk[:, pl.ds(pl.multiple_of((1 - par) * 256, 256), 256)] = aux_pair[...]

    @pl.when(f == 0)
    def _():
        wq[...] = main[...]
        wv[...] = main_in[...]

    @pl.when(f == 1)
    def _():
        wq[...] = main_in[...]
        wv[...] = main[...]


def request_kernel(owner, rows_in, table, slot, owners, rows, sems):
    first = pltpu.make_async_copy(owner, owners, sems.at[0])
    second = pltpu.make_async_copy(rows_in, rows, sems.at[1])
    first.start()
    second.start()
    first.wait()
    second.wait()
    orow = owners[...]
    above = lax.broadcasted_iota(jnp.int32, (ROWS, ROWS), 0)
    along = lax.broadcasted_iota(jnp.int32, (ROWS, ROWS), 1)
    ocol = jnp.sum(jnp.where(above == along, orow, 0), axis=1, keepdims=True)
    same = ocol == orow
    rank = jnp.sum(jnp.where(same & (above < along), 1, 0), axis=0, keepdims=True)
    rank_col = jnp.sum(jnp.where(same & (along < above), 1, 0), axis=1, keepdims=True)
    mine = lax.broadcasted_iota(jnp.int32, (OWNERS, ROWS), 0) == orow
    lane = lax.broadcasted_iota(jnp.int32, (OWNERS, 128), 1)
    out = jnp.zeros((OWNERS, 128), jnp.int32)
    for k in range(SLOTS):
        column = jnp.sum(jnp.where(mine & (rank == k), rows[...], 0), axis=1, keepdims=True)
        out = jnp.where(lane == k, column, out)
    table[...] = out
    slot[...] = ocol * SLOTS + rank_col


def norm_kernel(first, fetched, slot, dna, gain, normed, staged, sem):
    rows = ROWS - first
    copy = pltpu.make_async_copy(dna.at[pl.ds(first, rows), :], staged, sem)
    copy.start()
    index = slot[pl.ds(first, rows), :]
    pick = (lax.broadcasted_iota(jnp.int32, (rows, OWNERS * SLOTS), 1) == index).astype(f32).astype(bf16)
    site = jnp.dot(pick, fetched[...], preferred_element_type=f32)
    copy.wait()
    resid = staged[...].astype(f32) + site
    mean = jnp.mean(resid * resid, axis=1, keepdims=True)
    normed[...] = (resid * lax.rsqrt(mean + EPSILON) * gain[...]).astype(bf16)


def conv_kernel(normed, rim, taps, out, padded):
    padded[pl.ds(0, 8), :] = rim[...].astype(f32)
    padded[pl.ds(8, ROWS), :] = normed[...].astype(f32)

    def column(c, carry):
        lanes = pl.ds(pl.multiple_of(c * 128, 128), 128)
        weight = taps[:, lanes].astype(f32)
        for part in range(2):
            total = jnp.zeros((128, 128), f32)
            for tap in range(7):
                total = total + weight[tap : tap + 1] * padded[pl.ds(part * 128 + 8 - tap, 128), lanes]
            out[pl.ds(part * 128, 128), lanes] = total.astype(bf16)
        return carry

    lax.fori_loop(0, D // 128, column, 0)


def q_kernel(own, other, wq, q):
    par = lax.rem(lax.axis_index("seq"), 2)
    for x, side in ((own, par), (other, 1 - par)):
        at = pl.ds(pl.multiple_of(side * ROWS, ROWS), ROWS)
        q[at, :] = jnp.dot(x[...], wq[...], preferred_element_type=f32).astype(bf16)


def blocks_of(k):
    if k == 0:
        return ((0, 0, 1), (1, 0, 0), (1, 1, 1))
    if k == HOPS:
        return ((0, 0, 2), (0, 1, 0), (1, 1, 2))
    return ((0, 0, 0), (0, 1, 0), (1, 0, 0), (1, 1, 0))


def score_block(k, own, other, wk, wv, q_ref, v_ref, e_ref, top_ref, sum_ref, k_ref, sc0, sc1):
    par = lax.rem(lax.axis_index("seq"), 2)
    for x, side in ((own, par), (other, 1 - par)):
        at = pl.ds(pl.multiple_of(side * ROWS, ROWS), ROWS)
        k_ref[at, :] = jnp.dot(x[...], wk[...], preferred_element_type=f32).astype(bf16)
        v_ref[at, :] = jnp.dot(x[...], wv[...], preferred_element_type=f32).astype(bf16)
    row = lax.broadcasted_iota(jnp.int32, (ROWS, ROWS), 0)
    col = lax.broadcasted_iota(jnp.int32, (ROWS, ROWS), 1)
    lane = lax.broadcasted_iota(jnp.int32, (ROWS, 128), 1)
    blocks = blocks_of(k)
    count = len(blocks)
    top_ref[...] = jnp.zeros((2, ROWS, 128), f32)
    sum_ref[...] = jnp.zeros((2, ROWS, 128), f32)

    def scores(hp, side, sc):
        lanes = pl.ds(pl.multiple_of(hp * 128, 128), 128)
        tops = [None, None]
        for i, (qb, half, edge) in enumerate(blocks):
            q = q_ref[qb * ROWS : (qb + 1) * ROWS, lanes]
            q = jnp.where((lane < HEAD) == (side == 0), q, jnp.zeros_like(q))
            keys = k_ref[half * ROWS : (half + 1) * ROWS, lanes]
            s = lax.dot_general(q, keys, (((1,), (1,)), ((), ())), preferred_element_type=f32)
            if edge:
                s = jnp.where(col <= row if edge == 1 else col > row, s, MASKED)
            sc[i] = s
            part = jnp.maximum(s[:, :128], s[:, 128:])
            tops[qb] = part if tops[qb] is None else jnp.maximum(tops[qb], part)
        return tuple(jnp.max(top, axis=1, keepdims=True) for top in tops)

    def weigh(h, sc, tops):
        for qb in range(2):
            total = None
            for i, (which, half, edge) in enumerate(blocks):
                if which == qb:
                    e = jnp.exp2((sc[i] - tops[qb]) * SCALE)
                    e_ref[pl.ds(pl.multiple_of((h * count + i) * ROWS, ROWS), ROWS), :] = e
                    part = e[:, :128] + e[:, 128:]
                    total = part if total is None else total + part
            total = jnp.sum(total, axis=1, keepdims=True)
            top_ref[qb] = jnp.where(lane == h, tops[qb], top_ref[qb])
            sum_ref[qb] = jnp.where(lane == h, total, sum_ref[qb])

    def pair(hp, even):
        odd = scores(hp, 1, sc1)
        weigh(2 * hp, sc0, even)
        after_it = scores(jnp.minimum(hp + 1, 3), 0, sc0)
        weigh(2 * hp + 1, sc1, odd)
        return after_it

    lax.fori_loop(0, 4, pair, scores(0, 0, sc0))


def attend_kernel(*refs):
    q_ref, own, other, wk, wv = refs[:5]
    values, es, tops, sums = (refs[5 + HOPS * i : 5 + HOPS * (i + 1)] for i in range(4))
    mine, theirs, v_last, e_last, top_last, sum_last, k_last, sc0, sc1, factor, done = refs[5 + 4 * HOPS :]
    score_block(HOPS, own, other, wk, wv, q_ref, v_last, e_last, top_last, sum_last, k_last, sc0, sc1)
    values, es = values + (v_last,), es + (e_last,)
    tops, sums = tops + (top_last,), sums + (sum_last,)
    seq = lax.axis_index("seq")
    par = lax.rem(seq, 2)
    chip = seq // 2
    lane = lax.broadcasted_iota(jnp.int32, (ROWS, 128), 1)
    for qb in range(2):
        top = tops[0][qb]
        for k in range(1, HOPS + 1):
            top = jnp.where(chip >= k, jnp.maximum(top, tops[k][qb]), top)
        total = jnp.zeros((ROWS, 128), f32)
        for k in range(HOPS + 1):
            weight = jnp.exp2((tops[k][qb] - top) * SCALE)
            weight = jnp.where(chip >= k, weight, 0.0)
            factor[qb, k] = weight
            total = total + weight * sums[k][qb]
        inverse = 1.0 / jnp.where(lane < 8, total, 1.0)
        for k in range(HOPS + 1):
            factor[qb, k] = factor[qb, k] * inverse

    def pair(hp, carry):
        lanes = pl.ds(pl.multiple_of(hp * 128, 128), 128)
        for qb in range(2):
            outs = []
            for side in range(2):
                h = 2 * hp + side
                acc = None
                for k in range(HOPS + 1):
                    blocks = blocks_of(k)
                    column = jnp.sum(jnp.where(lane == h, factor[qb, k], 0.0), axis=1, keepdims=True)
                    for i, (which, half, edge) in enumerate(blocks):
                        if which == qb:
                            at = pl.ds(pl.multiple_of((h * len(blocks) + i) * ROWS, ROWS), ROWS)
                            p = (es[k][at, :] * column).astype(bf16)
                            value = values[k][half * ROWS : (half + 1) * ROWS, lanes]
                            part = jnp.dot(p, value, preferred_element_type=f32)
                            acc = part if acc is None else acc + part
                outs.append(acc)
            done[qb, :, lanes] = jnp.where(lane < HEAD, outs[0], outs[1])
        return carry

    lax.fori_loop(0, 4, pair, 0)
    mine[...] = done[par]
    theirs[...] = done[1 - par]


def out_kernel(mine, received, gain, w_here, w_mine, w_other, out):
    par = lax.rem(lax.axis_index("seq"), 2)
    f = lax.axis_index("fsdp")
    a, b = mine[...], received[...]
    mean = (jnp.sum(a * a, axis=1, keepdims=True) + jnp.sum(b * b, axis=1, keepdims=True)) / D
    scale = lax.rsqrt(mean + EPSILON)
    at_a = pl.ds(pl.multiple_of(par * HALF, HALF), HALF)
    at_b = pl.ds(pl.multiple_of((1 - par) * HALF, HALF), HALF)
    na = (a * scale * gain[:, at_a]).astype(bf16)
    nb = (b * scale * gain[:, at_b]).astype(bf16)
    here = jnp.dot(na, w_here[at_a, :], preferred_element_type=f32)
    here = here + jnp.dot(nb, w_here[at_b, :], preferred_element_type=f32)
    there = jnp.dot(na, w_mine[...], preferred_element_type=f32)
    there = there + jnp.dot(nb, w_other[...], preferred_element_type=f32)
    out[:, pl.ds(pl.multiple_of(f * HALF, HALF), HALF)] = here.astype(bf16)
    out[:, pl.ds(pl.multiple_of((1 - f) * HALF, HALF), HALF)] = there.astype(bf16)


def local(dna_embed, site_owner, site_row, variant_table, norm_gain, conv_weight, qkv_weight, out_weight, attn_gain):
    count = lax.axis_size("seq")
    across = [(0, 1), (1, 0)]
    beyond = [(i, i ^ (count + 1)) for i in range(2 * count)]
    swap = [(i, i ^ 1) for i in range(count)]
    ahead = [(i, i + 2) for i in range(count - 2)]

    main, aux, half, keys = pl.pallas_call(
        slab_kernel,
        out_shape=(
            jax.ShapeDtypeStruct((D, HALF), bf16),
            jax.ShapeDtypeStruct((D, 256), bf16),
            jax.ShapeDtypeStruct((HALF, HALF), bf16),
            jax.ShapeDtypeStruct((D, HALF), bf16),
        ),
        in_specs=[anywhere()] * 2,
        out_specs=(vmem(),) * 4,
        scratch_shapes=[pltpu.SemaphoreType.DMA((4,))],
        compiler_params=limit(6),
        name="slabs",
    )(*(pltpu.with_memory_space_constraint(w, pltpu.HBM) for w in (qkv_weight, out_weight)))
    main_in = lax.ppermute(main, "fsdp", across)
    aux_in = lax.ppermute(aux, ("seq", "fsdp"), beyond)
    out_in = lax.ppermute(half, ("seq", "fsdp"), beyond)
    aux_pair = lax.ppermute(aux_in, "seq", swap)
    out_pair = lax.ppermute(out_in, "seq", swap)

    table, slot = pl.pallas_call(
        request_kernel,
        out_shape=(jax.ShapeDtypeStruct((OWNERS, 128), jnp.int32), jax.ShapeDtypeStruct((ROWS, 1), jnp.int32)),
        in_specs=[anywhere()] * 2,
        out_specs=(vmem(), vmem()),
        scratch_shapes=[pltpu.VMEM((1, ROWS), jnp.int32)] * 2 + [pltpu.SemaphoreType.DMA((2,))],
        compiler_params=limit(4),
        name="requests",
    )(*(pltpu.with_memory_space_constraint(v, pltpu.HBM) for v in (site_owner.reshape(1, ROWS), site_row)))
    wanted = lax.all_to_all(table, "seq", split_axis=0, concat_axis=0, tiled=True)
    found = variant_table[wanted[:, :SLOTS].reshape(OWNERS * SLOTS)]
    fetched = lax.all_to_all(found, "seq", split_axis=0, concat_axis=0, tiled=True)

    def norm(first):
        return pl.pallas_call(
            functools.partial(norm_kernel, first),
            out_shape=jax.ShapeDtypeStruct((ROWS - first, D), bf16),
            in_specs=[vmem(), vmem(), anywhere(), vmem()],
            out_specs=vmem(),
            scratch_shapes=[pltpu.VMEM((ROWS - first, D), bf16), pltpu.SemaphoreType.DMA],
            compiler_params=limit(10),
            name="norm",
        )(fetched, slot, pltpu.with_memory_space_constraint(dna_embed[0], pltpu.HBM), norm_gain.reshape(1, D))

    edge = norm(ROWS - 8)
    normed = norm(0)
    rim = lax.ppermute(edge, "seq", [(i, i + 1) for i in range(count - 1)])
    x = pl.pallas_call(
        conv_kernel,
        out_shape=jax.ShapeDtypeStruct((ROWS, D), bf16),
        in_specs=[vmem()] * 3,
        out_specs=vmem(),
        scratch_shapes=[pltpu.VMEM((ROWS + 8, D), f32)],
        compiler_params=limit(6),
        name="conv",
    )(normed, rim, conv_weight)
    own = [x]
    for _ in range(HOPS - 1):
        own.append(lax.ppermute(own[-1], "seq", ahead))
    ring, reach = 2 * Z, 2 * HOPS
    behind = [i // ring * ring + (i - 6) % ring for i in range(count - reach)]
    far = lax.ppermute(x, "seq", list(enumerate(behind)))
    own.append(lax.ppermute(far, "seq", [(b, i + reach) for i, b in enumerate(behind)]))
    other = []
    for hop in range(HOPS + 1):
        other.append(lax.ppermute(own[hop], "seq", swap))

    wq, wk, wv = pl.pallas_call(
        weight_kernel,
        out_shape=(jax.ShapeDtypeStruct((D, HALF), bf16),) * 3,
        in_specs=[vmem()] * 5,
        out_specs=(vmem(), vmem(), vmem()),
        compiler_params=limit(8),
        cost_estimate=cost(10**6, 6 * 2**20),
        name="weights",
    )(keys, main, main_in, aux_in, aux_pair)
    q = pl.pallas_call(
        q_kernel,
        out_shape=jax.ShapeDtypeStruct((2 * ROWS, HALF), bf16),
        in_specs=[vmem()] * 3,
        out_specs=vmem(),
        cost_estimate=cost(2 * 512 * D * HALF, 3 * 2**20),
        compiler_params=limit(6),
    name="queries",
    )(x, other[0], wq)

    def stats():
        return jax.ShapeDtypeStruct((2, ROWS, 128), f32)

    found = []
    for hop in range(HOPS):
        size = len(blocks_of(hop)) * 8 * ROWS
        found.append(
            pl.pallas_call(
                functools.partial(score_block, hop),
                out_shape=(
                    jax.ShapeDtypeStruct((2 * ROWS, HALF), bf16),
                    jax.ShapeDtypeStruct((size, ROWS), f32),
                    stats(),
                    stats(),
                ),
                in_specs=[vmem()] * 5,
                out_specs=(vmem(),) * 4,
                scratch_shapes=[pltpu.VMEM((2 * ROWS, HALF), bf16)] + [pltpu.VMEM((4, ROWS, ROWS), f32)] * 2,
                compiler_params=limit(5),
                cost_estimate=cost(2 * 10**9, 4 * 2**20),
                name="near",
            )(own[hop], other[hop], wk, wv, q)
        )
    mine, theirs = pl.pallas_call(
        attend_kernel,
        out_shape=(jax.ShapeDtypeStruct((ROWS, HALF), f32), jax.ShapeDtypeStruct((ROWS, HALF), f32)),
        in_specs=[vmem()] * (5 + 4 * HOPS),
        out_specs=(vmem(), vmem()),
        scratch_shapes=[
            pltpu.VMEM((2 * ROWS, HALF), bf16),
            pltpu.VMEM((len(blocks_of(HOPS)) * 8 * ROWS, ROWS), f32),
            pltpu.VMEM((2, ROWS, 128), f32),
            pltpu.VMEM((2, ROWS, 128), f32),
            pltpu.VMEM((2 * ROWS, HALF), bf16),
            pltpu.VMEM((4, ROWS, ROWS), f32),
            pltpu.VMEM((4, ROWS, ROWS), f32),
            pltpu.VMEM((2, HOPS + 1, ROWS, 128), f32),
            pltpu.VMEM((2, ROWS, HALF), f32),
        ],
        compiler_params=limit(15),
        cost_estimate=cost(5 * 10**9, 6 * 2**20),
        name="attend",
    )(q, own[HOPS], other[HOPS], wk, wv, *(found[k][i] for i in range(4) for k in range(HOPS)))
    received = lax.ppermute(theirs, "seq", swap)
    mixed = pl.pallas_call(
        out_kernel,
        out_shape=jax.ShapeDtypeStruct((ROWS, D), bf16),
        in_specs=[vmem()] * 6,
        out_specs=vmem(),
        compiler_params=limit(10),
        name="project",
    )(mine, received, attn_gain.reshape(1, D), out_weight, out_in, out_pair)
    return mixed[None]


def solution(mesh):
    in_specs = (
        P("fsdp", "seq", None),
        P("fsdp", "seq", None),
        P("fsdp", "seq"),
        P("seq", None),
        P(),
        P(),
        P(None, "fsdp"),
        P(None, "fsdp"),
        P(),
    )

    return jax.shard_map(local, mesh=mesh, in_specs=in_specs, out_specs=P("fsdp", "seq", None), check_vma=False)
```
